32 devices in a mesh: wide: 4 (over z), narrow: 8 (over y, x, core).
Axes of the slice: x: 2, y: 2, z: 4, core: 2. Of those that a mesh axis runs over, the one named last changes fastest.
Arguments:
- kernel: bfloat16 [2048, 2048], P('wide', 'narrow'), may hold values from -0.15625 to 0.15625
- hamiltonian: bfloat16 [2048, 2048], P('wide', 'narrow'), may hold values from -6 to 6
- kernel_tiles: int32 [32, 32], P('wide', 'narrow'), may hold values from 0 to 1, as said below
- ham_tiles: int32 [32, 32], P('wide', 'narrow'), may hold values from 0 to 1, as said below
- pair_row: int32 [2048], P(('wide', 'narrow')), may hold values from 0 to 7
- pair_col: int32 [2048], P(('wide', 'narrow')), may hold values from 0 to 3
- sphere_phi: bfloat16 [2048, 64, 512], P(('wide', 'narrow')), may hold values from -0.09375 to 0.09375
- owner: int32 [8, 4], P('narrow'), may hold values from 0 to 3, each once within a row
Outputs:
- gradient: float32 [32, 64, 512], P(('wide', 'narrow'))
The draws below stay inside these ranges and needn't reach their ends.
Inputs may be any that keep to these rules, and one draw needn't show every extreme that they name: Each row of owner is a permutation of 0 to 3. `kernel_tiles`: in each tile row, at most 4 ones fall among one narrow index's 4 tile columns, and some row has that many. `ham_tiles`: in each tile column, at most 7 ones fall among one wide index's 8 tile rows, and some column has that many.
All inputs are finite; a program needn't handle non-finite values.
Results may differ from the reference program's by a relative error of at most 0.0029.
Values may be sent and summed in bfloat16 or wider, within the bound.
A program may use at most 128 MiB of HBM per device.

```python
import jax
import jax.numpy as jnp
from jax import lax

TILE = 64
PTS = 512
BAND = 12
PAIR_DEV = 64
DEVICES_ATOMS = 32
MAT = 2048
TR_DEV = 8
TC_DEV = 4
PAIRS = 2048
N_WIDE = 4
N_NARROW = 8
DEVICES = 32


def wire_position(tile_ids):
    return tile_ids % TR_DEV * N_WIDE + tile_ids // TR_DEV


def tile_mask(key, salt):
    base = jax.random.fold_in(key, salt)
    tile_ids = jnp.arange(DEVICES_ATOMS, dtype=jnp.int32)
    position = wire_position(tile_ids)
    spread = jnp.abs(position[:, None] - position[None, :])
    distance = jnp.minimum(spread, DEVICES_ATOMS - spread)
    coin_flip = jax.random.randint(base, (DEVICES_ATOMS, DEVICES_ATOMS), 0, 2)
    full_band = (position[:, None] % 16 == 0) | (position[None, :] % 16 == 0)
    keep_tile = (distance <= BAND - 4) | (distance <= BAND) & ((coin_flip == 1) | full_band)
    return keep_tile.astype(jnp.int32)


def draw_kernel_tiles(key, part):
    return tile_mask(key, 101)


def draw_ham_tiles(key, part):
    return tile_mask(key, 202)


def pair_draw(key):
    base = jax.random.fold_in(key, 303)
    pair_ids = jnp.arange(PAIRS, dtype=jnp.int32)
    device_ids = pair_ids // PAIR_DEV
    wide_ids = device_ids // N_NARROW
    narrow_ids = device_ids % N_NARROW
    column = jax.random.randint(jax.random.fold_in(base, 1), (PAIRS,), 0, TC_DEV)
    column_tile = narrow_ids * TC_DEV + column
    column_pos = wire_position(column_tile)
    nearest = (column_pos - wide_ids) % DEVICES_ATOMS // N_WIDE
    offset = jax.random.randint(jax.random.fold_in(base, 2), (PAIRS,), -2, 3)
    row_local = (nearest + offset) % TR_DEV
    return (row_local.astype(jnp.int32), column.astype(jnp.int32))


def draw_pair_row(key, part):
    return pair_draw(key)[0]


def draw_pair_col(key, part):
    return pair_draw(key)[1]


def shard_levels(own_key, dims, split, least, largest):
    def one(axis_at, parts):
        steps = jax.random.uniform(jax.random.fold_in(jax.random.fold_in(own_key, 6), axis_at), (parts,), jnp.float32, least / len(split), largest / len(split))
        return jnp.repeat(jnp.exp(steps), dims[axis_at] // parts).reshape((-1,) + (1,) * (len(dims) - axis_at - 1))

    level = one(*split[0])
    for cut in split[1:]:
        level = level * one(*cut)
    return level


def centred(own_key, extent, scale, bound, split=(), held_as=jnp.bfloat16):
    level = shard_levels(own_key, extent, split, -0.22, 0.18) if split else 1.0
    array = jax.random.normal(own_key, extent, jnp.float32) * scale * level
    return jnp.minimum(jnp.maximum(array, -bound), bound).astype(held_as)


def setup_inputs(seed: int = 0) -> dict:
    streams_of = jax.random.split(jax.random.key(seed), 9)
    kernel = centred(streams_of[0], (MAT, MAT), (TILE * 2 * BAND) ** -0.5, 0.15625, ((0, 4), (1, 8)))
    hamiltonian = centred(streams_of[1], (MAT, MAT), 1.0, 6.0, ((0, 4), (1, 8)))
    kernel_tiles = draw_kernel_tiles(jax.random.fold_in(streams_of[8], 71), 0)
    ham_tiles = draw_ham_tiles(jax.random.fold_in(streams_of[8], 71), 0)
    pair_row = draw_pair_row(jax.random.fold_in(streams_of[8], 71), 0)
    pair_col = draw_pair_col(jax.random.fold_in(streams_of[8], 71), 0)
    sphere_phi = centred(streams_of[6], (PAIRS, TILE, PTS), (TILE * PAIR_DEV) ** -0.5, 0.09375, ((0, 32),))
    owner = jax.vmap(lambda own: jax.random.permutation(own, TC_DEV))(jax.random.split(streams_of[7], TR_DEV)).reshape((TR_DEV, TC_DEV)).astype(jnp.int32)
    return {"kernel": kernel, "hamiltonian": hamiltonian, "kernel_tiles": kernel_tiles, "ham_tiles": ham_tiles, "pair_row": pair_row, "pair_col": pair_col, "sphere_phi": sphere_phi, "owner": owner}


def expand(mask_tiles, tile_width):
    return jnp.repeat(jnp.repeat(mask_tiles, tile_width, axis=0), tile_width, axis=1)


def reference(kernel, hamiltonian, kernel_tiles, ham_tiles, pair_row, pair_col, sphere_phi, owner):
    kmasked = kernel * expand(kernel_tiles, TILE).astype(jnp.bfloat16)
    hmasked = hamiltonian * expand(ham_tiles, TILE).astype(jnp.bfloat16)
    coefficients = jnp.dot(kmasked, hmasked, preferred_element_type=jnp.float32).astype(jnp.bfloat16)
    tile_count = MAT // TILE
    tile_table = coefficients.reshape(tile_count, TILE, tile_count, TILE).transpose(0, 2, 1, 3)
    device_ids = jnp.arange(DEVICES, dtype=jnp.int32)
    wide_ids = device_ids // N_NARROW
    narrow_ids = device_ids % N_NARROW
    row_groups = pair_row.reshape(DEVICES, PAIR_DEV)
    col_groups = pair_col.reshape(DEVICES, PAIR_DEV)
    phi_groups = sphere_phi.reshape(DEVICES, PAIR_DEV, TILE, PTS)

    def one_device(running, inputs):
        wide_id, narrow_id, rows_here, cols_here, phi_here = inputs
        block_rows = (wide_id * TR_DEV + rows_here).astype(jnp.int32)
        block_cols = (narrow_id * TC_DEV + cols_here).astype(jnp.int32)
        chosen = tile_table[block_rows, block_cols].astype(jnp.float32)
        gradient_blocks = jnp.einsum("pij,pir->pjr", chosen, phi_here.astype(jnp.float32),
                                     precision=lax.Precision.HIGHEST)
        owners = owner[narrow_id, cols_here]
        slots = (owners * N_NARROW + narrow_id).astype(jnp.int32)
        running = running + jax.ops.segment_sum(gradient_blocks, slots, num_segments=DEVICES)
        return running, None

    starting = jnp.zeros((DEVICES, TILE, PTS), jnp.float32)
    gradient, _ = lax.scan(one_device, starting, (wide_ids, narrow_ids, row_groups, col_groups, phi_groups))
    return gradient
```

```python
import functools

import jax
import jax.numpy as jnp
from jax import lax
from jax.experimental import pallas as pl
from jax.experimental.pallas import tpu as pltpu
from jax.sharding import PartitionSpec as P

MESH = pl.DeviceIdType.MESH
NT = (((1,), (1,)), ((), ()))


def chunk_sizes(tile):
    return (tile // 2, tile // 4, tile // 4)


def xor(a, b, size):
    total, bit = 0, 1
    while bit < size:
        total = total + ((a // bit + b // bit) % 2) * bit
        bit *= 2
    return total


def kernel_body(
    n_wide, n_narrow, tile,
    ktiles_hbm, htiles_hbm, rows_hbm, cols_hbm, owner_hbm, k_hbm, h_hbm, phi_hbm, out_ref,
    ktiles, htiles, rows, cols, owner, k_in, h_in, h_fit, phi, kbuf, full0, full1, full2, pack0, pack1, pack2,
    acc, table, lhs, own, stage, landed,
    in_sem, k_send, k_recv, s_send, s_recv, h_send, h_recv, r_send, r_recv,
):
    z = lax.axis_index("wide")
    n = lax.axis_index("narrow")
    chips = n_narrow // 2
    chip, core = n // 2, n % 2
    tile_cols, tile_rows = htiles.shape
    height, kcols = k_hbm.shape
    hrows, breadth = h_hbm.shape
    per = hrows // kcols
    pairs = rows.shape[0]
    full, pack = (full0, full1, full2), (pack0, pack1, pack2)
    sizes = chunk_sizes(tile)
    firsts = [sum(sizes[:c]) for c in range(len(sizes))]
    lanes = 2 * tile
    blocks_full = tile_rows // 2 - 1
    tree = chips == 4
    hh = height // 2

    barrier = pltpu.get_barrier_semaphore()

    def at(w, m):
        return (w, m)

    def chip_at(g):
        return at(z, xor(chip, g, chips) * 2 + core)

    direct = (1, 2) if tree else tuple(range(1, chips))
    for g in direct:
        pl.semaphore_signal(barrier, inc=1, device_id=chip_at(g), device_id_type=MESH)
    pl.semaphore_signal(barrier, inc=1, device_id=at(z, chip * 2 + 1 - core), device_id_type=MESH)
    for s in range(1, n_wide):
        pl.semaphore_signal(barrier, inc=1, device_id=at((z + s) % n_wide, n), device_id_type=MESH)

    load_h = pltpu.make_async_copy(h_hbm, h_in, in_sem.at[0])
    load_k = pltpu.make_async_copy(k_hbm, k_in, in_sem.at[1])
    load_p = pltpu.make_async_copy(phi_hbm, phi, in_sem.at[2])
    tables = [
        pltpu.make_async_copy(a, b, in_sem.at[3 + i])
        for i, (a, b) in enumerate((
            (htiles_hbm, htiles), (ktiles_hbm, ktiles), (rows_hbm, rows), (cols_hbm, cols), (owner_hbm, owner)))
    ]
    tables[0].start()
    load_h.start()
    load_k.start()
    for load in tables[1:]:
        load.start()
    load_p.start()

    def bf(mask):
        return jnp.where(mask, 1.0, 0.0).astype(jnp.bfloat16)

    def spread(values, extent):
        lane_tile = lax.broadcasted_iota(jnp.int32, (1, extent), 1) // tile
        row = jnp.zeros((1, extent), jnp.int32)
        for a in range(tile_cols):
            row = jnp.where(lane_tile == a, values[a], row)
        return row

    def mask_rows(tiles, b, extent):
        return spread([tiles[a, b] for a in range(tile_cols)], extent).astype(jnp.float32).astype(jnp.bfloat16)

    def tile_span(b):
        return pl.ds(b * tile, tile)

    tables[0].wait()
    holes = []
    for a in range(tile_cols):
        run, count = htiles[a, 0], htiles[a, 0]
        for b in range(1, tile_rows):
            run = run * htiles[a, b]
            count = count + run
        holes.append(count)
    hole = spread(holes, breadth)
    hole_odd = bf(hole % 2 == 1)
    hole_even = bf(hole % 2 == 0)
    lane_half = lax.broadcasted_iota(jnp.int32, (1, breadth), 1) // (breadth // 2)
    halves = [bf(lane_half == 0), bf(lane_half == 1)]
    load_h.wait()
    last = []
    for b in (tile_rows - 2, tile_rows - 1):
        h_in[tile_span(b), :] = h_in[tile_span(b), :] * mask_rows(htiles, b, breadth)
        last.append(h_in[tile_span(b), :])
    left_over = last[0] * hole_odd + last[1] * hole_even
    h_fit[tile_span(tile_rows - 2), :] = left_over * halves[0]
    h_fit[tile_span(tile_rows - 1), :] = left_over * halves[1]
    for b in range(tile_rows - 2):
        value = h_in[tile_span(b), :] * mask_rows(htiles, b, breadth)
        h_in[tile_span(b), :] = value
        h_fit[tile_span(b), :] = value + last[b % 2] * bf(hole == b)

    def pick(c, rows_out):
        jc = sizes[c]
        r = lax.broadcasted_iota(jnp.int32, (rows_out, breadth), 0)
        col = lax.broadcasted_iota(jnp.int32, (rows_out, breadth), 1)
        return r // jc * tile + firsts[c] + r % jc, col

    def turn(which, x):
        return lax.dot_general(which, x, NT, preferred_element_type=jnp.float32).astype(jnp.bfloat16)

    def fold(c):
        size = tile_cols * sizes[c]
        want, col = pick(c, size)
        out = turn(bf(col == want), h_fit[:tile * (tile_rows - 2), :])
        for q in range(blocks_full):
            pack[c][z, q * size:(q + 1) * size, :] = out[:, q * lanes:(q + 1) * lanes]
        want, col = pick(c, size // 2)
        out = turn(bf((col == want) | (col == want + breadth // 2)), h_fit[tile * (tile_rows - 2):, :])
        pack[c][z, blocks_full * size:blocks_full * size + size // 2, :] = out
        if c == 0:
            row = lax.broadcasted_iota(jnp.int32, (16, lanes), 0)
            note = jnp.zeros((16, lanes), jnp.int32)
            for a in range(tile_cols):
                note = jnp.where(row == a, holes[a], note)
            pack[0][z, blocks_full * size + size // 2:, :] = note.astype(jnp.float32).astype(jnp.bfloat16)

    def fill_own(c):
        want, col = pick(c, tile_cols * sizes[c])
        full[c][z] = turn(bf(col == want), h_in[...])

    def unfold(c, w):
        jc = sizes[c]
        size = tile_cols * jc
        notes = pack[0][w, blocks_full * tile_cols * sizes[0] + tile_cols * sizes[0] // 2:, :].astype(jnp.float32)
        side = lax.broadcasted_iota(jnp.int32, (1, lanes), 1) // tile
        sidef = side.astype(jnp.float32)
        lone = pack[c][w, blocks_full * size:blocks_full * size + size // 2, :]
        swapped = pltpu.roll(lone.astype(jnp.float32), tile, 1).astype(jnp.bfloat16)
        for a in range(tile_cols):
            gap = notes[a:a + 1, :]
            gap_odd = sum(bf(gap == 2 * i + 1) for i in range(tile_rows // 2))
            gap_even = sum(bf(gap == 2 * i) for i in range(tile_rows // 2))
            span = pl.ds(a * jc, jc)
            moved = None
            for q in range(blocks_full):
                x = pack[c][w, q * size + a * jc:q * size + (a + 1) * jc, :]
                hit = gap == sidef + 2 * q
                full[c][w, span, q * lanes:(q + 1) * lanes] = x * bf(~hit)
                part = x * bf(hit)
                moved = part if moved is None else moved + part
            group = a // (tile_cols // 2)
            inner = a % (tile_cols // 2) * jc
            there, here = lone[inner:inner + jc], swapped[inner:inner + jc]
            to_left, to_right = (there, here) if group == 0 else (here, there)
            moved = moved + to_left * (gap_odd * bf(side == 0)) + to_right * (gap_even * bf(side == 1))
            full[c][w, span, blocks_full * lanes:] = moved

    fold(0)
    pl.semaphore_wait(barrier, len(direct) + 1 + n_wide - 1)

    def h_copy(u, way, s, src):
        ref = pack[u].at[src]
        return pltpu.make_async_remote_copy(
            src_ref=ref, dst_ref=ref, send_sem=h_send.at[u, way, s], recv_sem=h_recv.at[u, way, s],
            device_id=at(z + 1 if way == 0 else z - 1, n), device_id_type=MESH)

    def source(way, s):
        return z - s if way == 0 else z + s

    def has_next(way):
        return z < n_wide - 1 if way == 0 else z > 0

    def has_source(way, s):
        return z >= s if way == 0 else z < n_wide - s

    def h_own(u):
        for way in range(2):
            @pl.when(has_next(way))
            def _():
                h_copy(u, way, 0, z).start()

    def h_pass(u, s):
        for way in range(2):
            @pl.when(has_source(way, s) & has_next(way))
            def _():
                h_copy(u, way, s - 1, source(way, s)).wait_recv()
                h_copy(u, way, s, source(way, s)).start()

    def h_keep(u, s):
        for way in range(2):
            @pl.when(has_source(way, s) & (z == (n_wide - 1 if way == 0 else 0)))
            def _():
                h_copy(u, way, s - 1, source(way, s)).wait_recv()

    def slot(g, c, h):
        return kbuf.at[xor(chip, g, chips) * 2 + c, pl.ds(h * hh, hh)]

    def k_copy(g, h, held, to):
        ref = slot(held, core, h)
        return pltpu.make_async_remote_copy(
            src_ref=ref, dst_ref=ref, send_sem=k_send.at[g, h], recv_sem=k_recv.at[g, h],
            device_id=chip_at(to), device_id_type=MESH)

    def k_sent(g, h):
        return k_copy(g, h, 1 + h, 2 - h) if tree and g == 3 else k_copy(g, h, 0, g)

    def sib_copy(g, h, c):
        ref = slot(g, c, h)
        return pltpu.make_async_remote_copy(
            src_ref=ref, dst_ref=ref, send_sem=s_send.at[g, h], recv_sem=s_recv.at[g, h],
            device_id=at(z, chip * 2 + 1 - core), device_id_type=MESH)

    def k_arrive(g, h):
        k_copy(g, h, g, 1).wait_recv()
        if tree and g == 1 + h:
            k_sent(3, h).start()
        sib_copy(g, h, core).start()

    h_own(0)
    fold(1)
    h_own(1)
    tables[1].wait()
    load_k.wait()
    for b in range(tile_rows):
        kbuf[n, tile_span(b), :] = k_in[tile_span(b), :] * mask_rows(ktiles, b, kcols)
    order = ((1, 0), (2, 1), (1, 1), (2, 0)) if tree else tuple((g, h) for g in direct for h in range(2))
    for g, h in order:
        k_sent(g, h).start()
    for h in range(2):
        sib_copy(0, h, core).start()
    fold(2)
    for c in range(3):
        fill_own(c)

    h_pass(0, 1)
    for g, h in order[:2]:
        k_arrive(g, h)
    h_own(2)
    h_pass(1, 1)
    for g, h in order[2:]:
        k_arrive(g, h)
    for s in range(2, n_wide - 1):
        h_pass(0, s)
    h_pass(2, 1)
    for s in range(2, n_wide - 1):
        h_pass(1, s)
    if tree:
        for h in range(2):
            k_arrive(3, h)
    for s in range(2, n_wide - 1):
        h_pass(2, s)

    def accumulate(c, w):
        size = tile_cols * sizes[c]

        @pl.when(w != z)
        def _():
            unfold(c, w)

        total = acc[:size]
        for i in range(per):
            total = total + lax.dot_general(
                full[c][w, :, i * kcols:(i + 1) * kcols], kbuf[w * per + i], NT,
                preferred_element_type=jnp.float32)
        acc[:size] = total

    lane = lax.broadcasted_iota(jnp.int32, (1, lanes), 1)
    low = lane < tile

    def finish(c):
        jc, j0 = sizes[c], firsts[c]
        size = tile_cols * jc
        for b2 in range(tile_rows // 2):
            x = acc[:size, lanes * b2:lanes * (b2 + 1)].astype(jnp.bfloat16).astype(jnp.float32)
            y = pltpu.roll(x, tile, 1)
            for odd in range(2):
                both = jnp.where(low, x, y) if odd == 0 else jnp.where(low, y, x)
                for a in range(tile_cols):
                    table[(2 * b2 + odd) * tile_cols + a, :jc] = both[a * jc:(a + 1) * jc]

        def place(t, carry):
            c0, c1 = cols[2 * t], cols[2 * t + 1]
            first = table[rows[2 * t] * tile_cols + c0, :jc]
            second = table[rows[2 * t + 1] * tile_cols + c1, :jc]
            both = jnp.where(low, first, second)
            dest = jnp.where(low, owner[0, c0], owner[0, c1])
            at_lane = pl.ds(pl.multiple_of(t * lanes, lanes), lanes)
            for d in range(n_wide):
                lhs[d * jc:(d + 1) * jc, at_lane] = jnp.where(dest == d, both, 0.0).astype(jnp.bfloat16)
            return carry

        lax.fori_loop(0, pairs // 2, place, 0, unroll=4)
        blocks = jnp.dot(lhs[:n_wide * jc], phi[...], preferred_element_type=jnp.float32)
        for d in range(n_wide):
            piece = blocks[d * jc:(d + 1) * jc]
            own[d, j0:j0 + jc] = piece
            stage[d, j0:j0 + jc] = piece.astype(jnp.bfloat16)

    def r_copy(c, s):
        span = pl.ds(firsts[c], sizes[c])
        return pltpu.make_async_remote_copy(
            src_ref=stage.at[(z + s) % n_wide, span], dst_ref=landed.at[s - 1, span],
            send_sem=r_send.at[c, s - 1], recv_sem=r_recv.at[c, s - 1],
            device_id=at((z + s) % n_wide, n), device_id_type=MESH)

    def chunk(c):
        for s in range(1, n_wide - 1):
            h_keep(c, s)
        size = tile_cols * sizes[c]
        acc[:size] = jnp.zeros((size, height), jnp.float32)

        def step(w, carry):
            accumulate(c, w)
            return carry

        lax.fori_loop(z // (n_wide - 1), n_wide - (n_wide - 1 - z) // (n_wide - 1), step, 0)
        h_keep(c, n_wide - 1)

        @pl.when((z == 0) | (z == n_wide - 1))
        def _():
            accumulate(c, n_wide - 1 - z)

        finish(c)
        for s in range(1, n_wide):
            r_copy(c, s).start()

    for g in range(chips):
        for h in range(2):
            sib_copy(g, h, 1 - core).wait_recv()
    load_p.wait()
    for load in tables[2:]:
        load.wait()
    for c in range(3):
        chunk(c)

    for c in range(3):
        span = pl.ds(firsts[c], sizes[c])
        total = own[z, span, :]
        for s in range(1, n_wide):
            r_copy(c, s).wait_recv()
            total = total + landed[s - 1, span, :].astype(jnp.float32)
        out_ref[0, span, :] = total

    for c in range(3):
        for s in range(1, n_wide):
            r_copy(c, s).wait_send()
    for g in range(1, chips):
        for h in range(2):
            k_sent(g, h).wait_send()
    for g in range(chips):
        for h in range(2):
            sib_copy(g, h, core).wait_send()
    for u in range(3):
        for way in range(2):
            for s in range(n_wide - 1):
                @pl.when(has_next(way) & has_source(way, s))
                def _():
                    h_copy(u, way, s, source(way, s)).wait_send()


def body(n_wide, n_narrow, kernel, hamiltonian, kernel_tiles, ham_tiles, pair_row, pair_col, sphere_phi, owner):
    pairs, tile, pts = sphere_phi.shape
    height, kcols = kernel.shape
    hrows, breadth = hamiltonian.shape
    tile_rows, tile_cols = ham_tiles.shape
    chips = n_narrow // 2
    hbm = pl.BlockSpec(memory_space=pltpu.HBM)
    dma = pltpu.SemaphoreType.DMA
    sizes = chunk_sizes(tile)
    top = max(sizes)
    bf16 = jnp.bfloat16

    def packed(c):
        size = tile_cols * sizes[c]
        return (tile_rows // 2 - 1) * size + size // 2 + (16 if c == 0 else 0)

    return pl.pallas_call(
        functools.partial(kernel_body, n_wide, n_narrow, tile),
        out_shape=jax.ShapeDtypeStruct((1, tile, pts), jnp.float32),
        in_specs=[hbm] * 8,
        out_specs=pl.BlockSpec(memory_space=pltpu.VMEM),
        scratch_shapes=[
            pltpu.SMEM((tile_cols, tile_rows), jnp.int32),
            pltpu.SMEM((tile_cols, tile_rows), jnp.int32),
            pltpu.SMEM((pairs,), jnp.int32),
            pltpu.SMEM((pairs,), jnp.int32),
            pltpu.SMEM((1, tile_cols), jnp.int32),
            pltpu.VMEM((height, kcols), bf16),
            pltpu.VMEM((hrows, breadth), bf16),
            pltpu.VMEM((hrows, breadth), bf16),
            pltpu.VMEM((pairs * tile, pts), bf16),
            pltpu.VMEM((n_narrow, height, kcols), bf16),
            *[pltpu.VMEM((n_wide, tile_cols * size, hrows), bf16) for size in sizes],
            *[pltpu.VMEM((n_wide, packed(c), 2 * tile), bf16) for c in range(len(sizes))],
            pltpu.VMEM((tile_cols * top, height), jnp.float32),
            pltpu.VMEM((tile_rows * tile_cols, top, 2 * tile), jnp.float32),
            pltpu.VMEM((n_wide * top, pairs * tile), bf16),
            pltpu.VMEM((n_wide, tile, pts), jnp.float32),
            pltpu.VMEM((n_wide, tile, pts), bf16),
            pltpu.VMEM((n_wide - 1, tile, pts), bf16),
            dma((8,)),
            dma((chips, 2)), dma((chips, 2)),
            dma((chips, 2)), dma((chips, 2)),
            dma((3, 2, n_wide)), dma((3, 2, n_wide)),
            dma((3, n_wide)), dma((3, n_wide)),
        ],
        compiler_params=pltpu.CompilerParams(
            collective_id=0, has_side_effects=True, vmem_limit_bytes=60 * 2**20),
    )(kernel_tiles.T, ham_tiles.T, pair_row, pair_col, owner, kernel, hamiltonian,
      sphere_phi.reshape(pairs * tile, pts))


def solution(mesh):
    return jax.shard_map(
        functools.partial(body, mesh.shape["wide"], mesh.shape["narrow"]),
        mesh=mesh,
        in_specs=(
            P("wide", "narrow"),
            P("wide", "narrow"),
            P("wide", "narrow"),
            P("wide", "narrow"),
            P(("wide", "narrow")),
            P(("wide", "narrow")),
            P(("wide", "narrow"), None, None),
            P("narrow", None),
        ),
        out_specs=P(("wide", "narrow"), None, None),
        check_vma=False,
    )
```

```python
import functools

import jax
import jax.numpy as jnp
from jax import lax
from jax.experimental import pallas as pl
from jax.experimental.pallas import tpu as pltpu
from jax.sharding import PartitionSpec as P

MESH = pl.DeviceIdType.MESH
NT = (((1,), (1,)), ((), ()))


def chunk_sizes(tile):
    return (tile // 2, tile // 4, tile // 4)


def xor(a, b, size):
    total, bit = 0, 1
    while bit < size:
        total = total + ((a // bit + b // bit) % 2) * bit
        bit *= 2
    return total


def kernel_body(
    n_wide, n_narrow, tile,
    ktiles_hbm, htiles_hbm, rows_hbm, cols_hbm, owner_hbm, k_hbm, h_hbm, phi_hbm, out_ref,
    ktiles, htiles, rows, cols, owner, k_in, h_in, h_fit, phi, kbuf, full0, full1, full2, pack0, pack1, pack2,
    acc, table, lhs, own, stage, landed,
    in_sem, k_send, k_recv, s_send, s_recv, h_send, h_recv, r_send, r_recv,
):
    z = lax.axis_index("wide")
    n = lax.axis_index("narrow")
    chips = n_narrow // 2
    chip, core = n // 2, n % 2
    tile_cols, tile_rows = htiles.shape
    height, kcols = k_hbm.shape
    hrows, breadth = h_hbm.shape
    per = hrows // kcols
    pairs = rows.shape[0]
    full, pack = (full0, full1, full2), (pack0, pack1, pack2)
    sizes = chunk_sizes(tile)
    firsts = [sum(sizes[:c]) for c in range(len(sizes))]
    lanes = 2 * tile
    blocks_full = tile_rows // 2 - 1
    tree = chips == 4
    hh = kcols // 2

    barrier = pltpu.get_barrier_semaphore()

    def at(w, m):
        return (w, m)

    def chip_at(g):
        return at(z, xor(chip, g, chips) * 2 + core)

    direct = (1, 2) if tree else tuple(range(1, chips))
    for g in direct:
        pl.semaphore_signal(barrier, inc=1, device_id=chip_at(g), device_id_type=MESH)
    pl.semaphore_signal(barrier, inc=1, device_id=at(z, chip * 2 + 1 - core), device_id_type=MESH)
    for s in range(1, n_wide):
        pl.semaphore_signal(barrier, inc=1, device_id=at((z + s) % n_wide, n), device_id_type=MESH)

    load_h = pltpu.make_async_copy(h_hbm, h_in, in_sem.at[0])
    load_k = pltpu.make_async_copy(k_hbm, k_in, in_sem.at[1])
    load_p = pltpu.make_async_copy(phi_hbm, phi, in_sem.at[2])
    tables = [
        pltpu.make_async_copy(a, b, in_sem.at[3 + i])
        for i, (a, b) in enumerate((
            (htiles_hbm, htiles), (ktiles_hbm, ktiles), (rows_hbm, rows), (cols_hbm, cols), (owner_hbm, owner)))
    ]
    tables[0].start()
    load_h.start()
    load_k.start()
    for load in tables[1:]:
        load.start()
    load_p.start()

    def bf(mask):
        return jnp.where(mask, 1.0, 0.0).astype(jnp.bfloat16)

    def spread(values, extent):
        lane_tile = lax.broadcasted_iota(jnp.int32, (1, extent), 1) // tile
        row = jnp.zeros((1, extent), jnp.int32)
        for a in range(tile_cols):
            row = jnp.where(lane_tile == a, values[a], row)
        return row

    def mask_rows(tiles, b, extent):
        return spread([tiles[a, b] for a in range(tile_cols)], extent).astype(jnp.float32).astype(jnp.bfloat16)

    def tile_span(b):
        return pl.ds(b * tile, tile)

    tables[0].wait()
    holes = []
    for a in range(tile_cols):
        run, count = htiles[a, 0], htiles[a, 0]
        for b in range(1, tile_rows):
            run = run * htiles[a, b]
            count = count + run
        holes.append(count)
    hole = spread(holes, breadth)
    hole_odd = bf(hole % 2 == 1)
    hole_even = bf(hole % 2 == 0)
    lane_half = lax.broadcasted_iota(jnp.int32, (1, breadth), 1) // (breadth // 2)
    halves = [bf(lane_half == 0), bf(lane_half == 1)]
    load_h.wait()
    last = []
    for b in (tile_rows - 2, tile_rows - 1):
        h_in[tile_span(b), :] = h_in[tile_span(b), :] * mask_rows(htiles, b, breadth)
        last.append(h_in[tile_span(b), :])
    left_over = last[0] * hole_odd + last[1] * hole_even
    h_fit[tile_span(tile_rows - 2), :] = left_over * halves[0]
    h_fit[tile_span(tile_rows - 1), :] = left_over * halves[1]
    for b in range(tile_rows - 2):
        value = h_in[tile_span(b), :] * mask_rows(htiles, b, breadth)
        h_in[tile_span(b), :] = value
        h_fit[tile_span(b), :] = value + last[b % 2] * bf(hole == b)

    def pick(c, rows_out):
        jc = sizes[c]
        r = lax.broadcasted_iota(jnp.int32, (rows_out, breadth), 0)
        col = lax.broadcasted_iota(jnp.int32, (rows_out, breadth), 1)
        return r // jc * tile + firsts[c] + r % jc, col

    def turn(which, x):
        return lax.dot_general(which, x, NT, preferred_element_type=jnp.float32).astype(jnp.bfloat16)

    def fold(c):
        size = tile_cols * sizes[c]
        want, col = pick(c, size)
        out = turn(bf(col == want), h_fit[:tile * (tile_rows - 2), :])
        for q in range(blocks_full):
            pack[c][z, q * size:(q + 1) * size, :] = out[:, q * lanes:(q + 1) * lanes]
        want, col = pick(c, size // 2)
        out = turn(bf((col == want) | (col == want + breadth // 2)), h_fit[tile * (tile_rows - 2):, :])
        pack[c][z, blocks_full * size:blocks_full * size + size // 2, :] = out
        if c == 0:
            row = lax.broadcasted_iota(jnp.int32, (16, lanes), 0)
            note = jnp.zeros((16, lanes), jnp.int32)
            for a in range(tile_cols):
                note = jnp.where(row == a, holes[a], note)
            pack[0][z, blocks_full * size + size // 2:, :] = note.astype(jnp.float32).astype(jnp.bfloat16)

    def fill_own(c):
        want, col = pick(c, tile_cols * sizes[c])
        full[c][:, pl.ds(pl.multiple_of(z * hrows, hrows), hrows)] = turn(bf(col == want), h_in[...])

    def lane_block(w, q):
        return pl.ds(pl.multiple_of(w * hrows + q * lanes, lanes), lanes)

    def unfold(c, w):
        jc = sizes[c]
        size = tile_cols * jc
        notes = pack[0][w, blocks_full * tile_cols * sizes[0] + tile_cols * sizes[0] // 2:, :].astype(jnp.float32)
        side = lax.broadcasted_iota(jnp.int32, (1, lanes), 1) // tile
        sidef = side.astype(jnp.float32)
        lone = pack[c][w, blocks_full * size:blocks_full * size + size // 2, :]
        swapped = pltpu.roll(lone.astype(jnp.float32), tile, 1).astype(jnp.bfloat16)
        for a in range(tile_cols):
            gap = notes[a:a + 1, :]
            gap_odd = sum(bf(gap == 2 * i + 1) for i in range(tile_rows // 2))
            gap_even = sum(bf(gap == 2 * i) for i in range(tile_rows // 2))
            span = pl.ds(a * jc, jc)
            moved = None
            for q in range(blocks_full):
                x = pack[c][w, q * size + a * jc:q * size + (a + 1) * jc, :]
                hit = gap == sidef + 2 * q
                full[c][span, lane_block(w, q)] = x * bf(~hit)
                part = x * bf(hit)
                moved = part if moved is None else moved + part
            group = a // (tile_cols // 2)
            inner = a % (tile_cols // 2) * jc
            there, here = lone[inner:inner + jc], swapped[inner:inner + jc]
            to_left, to_right = (there, here) if group == 0 else (here, there)
            moved = moved + to_left * (gap_odd * bf(side == 0)) + to_right * (gap_even * bf(side == 1))
            full[c][span, lane_block(w, blocks_full)] = moved

    fold(0)
    pl.semaphore_wait(barrier, len(direct) + 1 + n_wide - 1)

    def h_copy(u, way, s, src):
        ref = pack[u].at[src]
        return pltpu.make_async_remote_copy(
            src_ref=ref, dst_ref=ref, send_sem=h_send.at[u, way, s], recv_sem=h_recv.at[u, way, s],
            device_id=at(z + 1 if way == 0 else z - 1, n), device_id_type=MESH)

    def source(way, s):
        return z - s if way == 0 else z + s

    def has_next(way):
        return z < n_wide - 1 if way == 0 else z > 0

    def has_source(way, s):
        return z >= s if way == 0 else z < n_wide - s

    def h_own(u):
        for way in range(2):
            @pl.when(has_next(way))
            def _():
                h_copy(u, way, 0, z).start()

    def h_pass(u, s):
        for way in range(2):
            @pl.when(has_source(way, s) & has_next(way))
            def _():
                h_copy(u, way, s - 1, source(way, s)).wait_recv()
                h_copy(u, way, s, source(way, s)).start()

    def h_keep(u, s):
        for way in range(2):
            @pl.when(has_source(way, s) & (z == (n_wide - 1 if way == 0 else 0)))
            def _():
                h_copy(u, way, s - 1, source(way, s)).wait_recv()

    def slot(g, c, h):
        return kbuf.at[pl.ds(pl.multiple_of((xor(chip, g, chips) * 2 + c) * kcols + h * hh, hh), hh)]

    def k_copy(g, h, held, to):
        ref = slot(held, core, h)
        return pltpu.make_async_remote_copy(
            src_ref=ref, dst_ref=ref, send_sem=k_send.at[g, h], recv_sem=k_recv.at[g, h],
            device_id=chip_at(to), device_id_type=MESH)

    def k_sent(g, h):
        return k_copy(g, h, 1 + h, 2 - h) if tree and g == 3 else k_copy(g, h, 0, g)

    def sib_copy(g, h, c):
        ref = slot(g, c, h)
        return pltpu.make_async_remote_copy(
            src_ref=ref, dst_ref=ref, send_sem=s_send.at[g, h], recv_sem=s_recv.at[g, h],
            device_id=at(z, chip * 2 + 1 - core), device_id_type=MESH)

    def k_arrive(g, h):
        k_copy(g, h, g, 1).wait_recv()
        if tree and g == 1 + h:
            k_sent(3, h).start()
        sib_copy(g, h, core).start()

    h_own(0)
    fold(1)
    h_own(1)
    tables[1].wait()
    load_k.wait()
    for b in range(tile_rows):
        k_in[tile_span(b), :] = k_in[tile_span(b), :] * mask_rows(ktiles, b, kcols)
    unit = lax.broadcasted_iota(jnp.int32, (kcols, kcols), 0) == lax.broadcasted_iota(jnp.int32, (kcols, kcols), 1)
    kbuf[pl.ds(pl.multiple_of(n * kcols, kcols), kcols), :] = turn(bf(unit), k_in[...])
    order = ((1, 0), (2, 1), (1, 1), (2, 0)) if tree else tuple((g, h) for g in direct for h in range(2))
    for g, h in order:
        k_sent(g, h).start()
    for h in range(2):
        sib_copy(0, h, core).start()
    fold(2)
    for c in range(3):
        fill_own(c)

    h_pass(0, 1)
    for g, h in order[:2]:
        k_arrive(g, h)
    h_own(2)
    h_pass(1, 1)
    for g, h in order[2:]:
        k_arrive(g, h)
    for s in range(2, n_wide - 1):
        h_pass(0, s)
    h_pass(2, 1)
    for s in range(2, n_wide - 1):
        h_pass(1, s)
    if tree:
        for h in range(2):
            k_arrive(3, h)
    for s in range(2, n_wide - 1):
        h_pass(2, s)

    first_near = z // (n_wide - 1)
    far = (n_wide - 1) * (1 - first_near)

    def product(c, w, count):
        span = pl.ds(pl.multiple_of(w * hrows, hrows), count * hrows)
        return jnp.dot(full[c][:, span], kbuf[span, :], preferred_element_type=jnp.float32)

    def ready(c):
        for s in range(1, n_wide - 1):
            h_keep(c, s)

        def step(w, carry):
            @pl.when(w != z)
            def _():
                unfold(c, w)

            return carry

        lax.fori_loop(first_near, first_near + n_wide - 1, step, 0)

    lane = lax.broadcasted_iota(jnp.int32, (1, lanes), 1)
    low = lane < tile

    def finish(c):
        jc, j0 = sizes[c], firsts[c]
        size = tile_cols * jc
        for b2 in range(tile_rows // 2):
            x = acc[:size, lanes * b2:lanes * (b2 + 1)].astype(jnp.bfloat16).astype(jnp.float32)
            y = pltpu.roll(x, tile, 1)
            for odd in range(2):
                both = jnp.where(low, x, y) if odd == 0 else jnp.where(low, y, x)
                for a in range(tile_cols):
                    table[(2 * b2 + odd) * tile_cols + a, :jc] = both[a * jc:(a + 1) * jc]

        def place(t):
            c0, c1 = cols[2 * t], cols[2 * t + 1]
            first = table[rows[2 * t] * tile_cols + c0, :jc]
            second = table[rows[2 * t + 1] * tile_cols + c1, :jc]
            both = jnp.where(low, first, second)
            dest = jnp.where(low, owner[0, c0], owner[0, c1])
            at_lane = pl.ds(t * lanes, lanes)
            for d in range(n_wide):
                lhs[d * jc:(d + 1) * jc, at_lane] = jnp.where(dest == d, both, 0.0).astype(jnp.bfloat16)

        for t in range(pairs // 2):
            place(t)
        blocks = jnp.dot(lhs[:n_wide * jc], phi[...], preferred_element_type=jnp.float32)
        for d in range(n_wide):
            piece = blocks[d * jc:(d + 1) * jc]
            own[d, j0:j0 + jc] = piece
            stage[d, j0:j0 + jc] = piece.astype(jnp.bfloat16)

    def r_copy(c, s):
        span = pl.ds(firsts[c], sizes[c])
        return pltpu.make_async_remote_copy(
            src_ref=stage.at[(z + s) % n_wide, span], dst_ref=landed.at[s - 1, span],
            send_sem=r_send.at[c, s - 1], recv_sem=r_recv.at[c, s - 1],
            device_id=at((z + s) % n_wide, n), device_id_type=MESH)

    def chunk(c):
        size = tile_cols * sizes[c]
        if c > 0:
            ready(c)
        acc[:size] = product(c, first_near, n_wide - 1)
        h_keep(c, n_wide - 1)
        unfold(c, far)
        acc[:size] += product(c, far, 1)
        finish(c)
        for s in range(1, n_wide):
            r_copy(c, s).start()

    ready(0)
    for g in range(chips):
        for h in range(2):
            sib_copy(g, h, 1 - core).wait_recv()
    load_p.wait()
    for load in tables[2:]:
        load.wait()
    for c in range(3):
        chunk(c)

    for c in range(3):
        span = pl.ds(firsts[c], sizes[c])
        total = own[z, span, :]
        for s in range(1, n_wide):
            r_copy(c, s).wait_recv()
            total = total + landed[s - 1, span, :].astype(jnp.float32)
        out_ref[0, span, :] = total

    for c in range(3):
        for s in range(1, n_wide):
            r_copy(c, s).wait_send()
    for g in range(1, chips):
        for h in range(2):
            k_sent(g, h).wait_send()
    for g in range(chips):
        for h in range(2):
            sib_copy(g, h, core).wait_send()
    for u in range(3):
        for way in range(2):
            for s in range(n_wide - 1):
                @pl.when(has_next(way) & has_source(way, s))
                def _():
                    h_copy(u, way, s, source(way, s)).wait_send()


def body(n_wide, n_narrow, kernel, hamiltonian, kernel_tiles, ham_tiles, pair_row, pair_col, sphere_phi, owner):
    pairs, tile, pts = sphere_phi.shape
    height, kcols = kernel.shape
    hrows, breadth = hamiltonian.shape
    tile_rows, tile_cols = ham_tiles.shape
    chips = n_narrow // 2
    hbm = pl.BlockSpec(memory_space=pltpu.HBM)
    dma = pltpu.SemaphoreType.DMA
    sizes = chunk_sizes(tile)
    top = max(sizes)
    bf16 = jnp.bfloat16

    def packed(c):
        size = tile_cols * sizes[c]
        return (tile_rows // 2 - 1) * size + size // 2 + (16 if c == 0 else 0)

    return pl.pallas_call(
        functools.partial(kernel_body, n_wide, n_narrow, tile),
        out_shape=jax.ShapeDtypeStruct((1, tile, pts), jnp.float32),
        in_specs=[hbm] * 8,
        out_specs=pl.BlockSpec(memory_space=pltpu.VMEM),
        scratch_shapes=[
            pltpu.SMEM((tile_cols, tile_rows), jnp.int32),
            pltpu.SMEM((tile_cols, tile_rows), jnp.int32),
            pltpu.SMEM((pairs,), jnp.int32),
            pltpu.SMEM((pairs,), jnp.int32),
            pltpu.SMEM((1, tile_cols), jnp.int32),
            pltpu.VMEM((height, kcols), bf16),
            pltpu.VMEM((hrows, breadth), bf16),
            pltpu.VMEM((hrows, breadth), bf16),
            pltpu.VMEM((pairs * tile, pts), bf16),
            pltpu.VMEM((n_narrow * kcols, height), bf16),
            *[pltpu.VMEM((tile_cols * size, n_wide * hrows), bf16) for size in sizes],
            *[pltpu.VMEM((n_wide, packed(c), 2 * tile), bf16) for c in range(len(sizes))],
            pltpu.VMEM((tile_cols * top, height), jnp.float32),
            pltpu.VMEM((tile_rows * tile_cols, top, 2 * tile), jnp.float32),
            pltpu.VMEM((n_wide * top, pairs * tile), bf16),
            pltpu.VMEM((n_wide, tile, pts), jnp.float32),
            pltpu.VMEM((n_wide, tile, pts), bf16),
            pltpu.VMEM((n_wide - 1, tile, pts), bf16),
            dma((8,)),
            dma((chips, 2)), dma((chips, 2)),
            dma((chips, 2)), dma((chips, 2)),
            dma((3, 2, n_wide)), dma((3, 2, n_wide)),
            dma((3, n_wide)), dma((3, n_wide)),
        ],
        compiler_params=pltpu.CompilerParams(
            collective_id=0, has_side_effects=True, vmem_limit_bytes=60 * 2**20),
    )(kernel_tiles.T, ham_tiles.T, pair_row, pair_col, owner, kernel, hamiltonian,
      sphere_phi.reshape(pairs * tile, pts))


def solution(mesh):
    return jax.shard_map(
        functools.partial(body, mesh.shape["wide"], mesh.shape["narrow"]),
        mesh=mesh,
        in_specs=(
            P("wide", "narrow"),
            P("wide", "narrow"),
            P("wide", "narrow"),
            P("wide", "narrow"),
            P(("wide", "narrow")),
            P(("wide", "narrow")),
            P(("wide", "narrow"), None, None),
            P("narrow", None),
        ),
        out_specs=P(("wide", "narrow"), None, None),
        check_vma=False,
    )
```

```python
import functools

import jax
import jax.numpy as jnp
from jax import lax
from jax.experimental import pallas as pl
from jax.experimental.pallas import tpu as pltpu
from jax.sharding import PartitionSpec as P

MESH = pl.DeviceIdType.MESH
NT = (((1,), (1,)), ((), ()))


def chunk_sizes(tile):
    return (tile // 2, tile // 4, tile // 4)


def xor(a, b, size):
    total, bit = 0, 1
    while bit < size:
        total = total + ((a // bit + b // bit) % 2) * bit
        bit *= 2
    return total


def kernel_body(
    n_wide, n_narrow, tile,
    ktiles_hbm, htiles_hbm, rows_hbm, cols_hbm, owner_hbm, k_hbm, h_hbm, phi_hbm, out_ref,
    ktiles, htiles, rows, cols, owner, k_in, h_in, h_fit, phi, kbuf, full0, full1, full2, pack0, pack1, pack2,
    acc, table, lhs, own, stage, landed,
    in_sem, k_send, k_recv, s_send, s_recv, h_send, h_recv, r_send, r_recv,
):
    z = lax.axis_index("wide")
    n = lax.axis_index("narrow")
    chips = n_narrow // 2
    chip, core = n // 2, n % 2
    tile_cols, tile_rows = htiles.shape
    height, kcols = k_hbm.shape
    hrows, breadth = h_hbm.shape
    per = hrows // kcols
    pairs = rows.shape[0]
    full, pack = (full0, full1, full2), (pack0, pack1, pack2)
    sizes = chunk_sizes(tile)
    firsts = [sum(sizes[:c]) for c in range(len(sizes))]
    lanes = 2 * tile
    blocks_full = tile_rows // 2 - 1
    tree = chips == 4
    hh = kcols // 2

    barrier = pltpu.get_barrier_semaphore()

    def at(w, m):
        return (w, m)

    def chip_at(g):
        return at(z, xor(chip, g, chips) * 2 + core)

    direct = (1, 2) if tree else tuple(range(1, chips))
    for g in direct:
        pl.semaphore_signal(barrier, inc=1, device_id=chip_at(g), device_id_type=MESH)
    pl.semaphore_signal(barrier, inc=1, device_id=at(z, chip * 2 + 1 - core), device_id_type=MESH)
    for way in range(2):
        @pl.when(z < n_wide - 1 if way == 0 else z > 0)
        def _():
            pl.semaphore_signal(barrier, inc=1, device_id=at(z + 1 - 2 * way, n), device_id_type=MESH)

    load_h = pltpu.make_async_copy(h_hbm, h_in, in_sem.at[0])
    load_k = pltpu.make_async_copy(k_hbm, k_in, in_sem.at[1])
    load_p = pltpu.make_async_copy(phi_hbm, phi, in_sem.at[2])
    tables = [
        pltpu.make_async_copy(a, b, in_sem.at[3 + i])
        for i, (a, b) in enumerate((
            (htiles_hbm, htiles), (ktiles_hbm, ktiles), (rows_hbm, rows), (cols_hbm, cols), (owner_hbm, owner)))
    ]
    tables[0].start()
    load_h.start()
    load_k.start()
    for load in tables[1:]:
        load.start()
    load_p.start()

    def bf(mask):
        return jnp.where(mask, 1.0, 0.0).astype(jnp.bfloat16)

    def spread(values, extent):
        lane_tile = lax.broadcasted_iota(jnp.int32, (1, extent), 1) // tile
        row = jnp.zeros((1, extent), jnp.int32)
        for a in range(tile_cols):
            row = jnp.where(lane_tile == a, values[a], row)
        return row

    def mask_rows(tiles, b, extent):
        return spread([tiles[a, b] for a in range(tile_cols)], extent).astype(jnp.float32).astype(jnp.bfloat16)

    def tile_span(b):
        return pl.ds(b * tile, tile)

    tables[0].wait()
    holes = []
    for a in range(tile_cols):
        run, count = htiles[a, 0], htiles[a, 0]
        for b in range(1, tile_rows):
            run = run * htiles[a, b]
            count = count + run
        holes.append(count)
    hole = spread(holes, breadth)
    hole_odd = bf(hole % 2 == 1)
    hole_even = bf(hole % 2 == 0)
    lane_half = lax.broadcasted_iota(jnp.int32, (1, breadth), 1) // (breadth // 2)
    halves = [bf(lane_half == 0), bf(lane_half == 1)]
    load_h.wait()
    last = []
    for b in (tile_rows - 2, tile_rows - 1):
        h_in[tile_span(b), :] = h_in[tile_span(b), :] * mask_rows(htiles, b, breadth)
        last.append(h_in[tile_span(b), :])
    left_over = last[0] * hole_odd + last[1] * hole_even
    h_fit[tile_span(tile_rows - 2), :] = left_over * halves[0]
    h_fit[tile_span(tile_rows - 1), :] = left_over * halves[1]
    for b in range(tile_rows - 2):
        value = h_in[tile_span(b), :] * mask_rows(htiles, b, breadth)
        h_in[tile_span(b), :] = value
        h_fit[tile_span(b), :] = value + last[b % 2] * bf(hole == b)

    def pick(c, rows_out):
        jc = sizes[c]
        r = lax.broadcasted_iota(jnp.int32, (rows_out, breadth), 0)
        col = lax.broadcasted_iota(jnp.int32, (rows_out, breadth), 1)
        return r // jc * tile + firsts[c] + r % jc, col

    def turn(which, x):
        return lax.dot_general(which, x, NT, preferred_element_type=jnp.float32).astype(jnp.bfloat16)

    def fold(c):
        size = tile_cols * sizes[c]
        want, col = pick(c, size)
        out = turn(bf(col == want), h_fit[:tile * (tile_rows - 2), :])
        for q in range(blocks_full):
            pack[c][z, q * size:(q + 1) * size, :] = out[:, q * lanes:(q + 1) * lanes]
        want, col = pick(c, size // 2)
        out = turn(bf((col == want) | (col == want + breadth // 2)), h_fit[tile * (tile_rows - 2):, :])
        pack[c][z, blocks_full * size:blocks_full * size + size // 2, :] = out
        if c == 0:
            row = lax.broadcasted_iota(jnp.int32, (16, lanes), 0)
            note = jnp.zeros((16, lanes), jnp.int32)
            for a in range(tile_cols):
                note = jnp.where(row == a, holes[a], note)
            pack[0][z, blocks_full * size + size // 2:, :] = note.astype(jnp.float32).astype(jnp.bfloat16)

    def fill_own(c):
        want, col = pick(c, tile_cols * sizes[c])
        full[c][:, pl.ds(pl.multiple_of(z * hrows, hrows), hrows)] = turn(bf(col == want), h_in[...])

    def lane_block(w, q):
        return pl.ds(pl.multiple_of(w * hrows + q * lanes, lanes), lanes)

    def unfold(c, w):
        jc = sizes[c]
        size = tile_cols * jc
        notes = pack[0][w, blocks_full * tile_cols * sizes[0] + tile_cols * sizes[0] // 2:, :].astype(jnp.float32)
        side = lax.broadcasted_iota(jnp.int32, (1, lanes), 1) // tile
        sidef = side.astype(jnp.float32)
        lone = pack[c][w, blocks_full * size:blocks_full * size + size // 2, :]
        swapped = pltpu.roll(lone.astype(jnp.float32), tile, 1).astype(jnp.bfloat16)
        for a in range(tile_cols):
            gap = notes[a:a + 1, :]
            gap_odd = sum(bf(gap == 2 * i + 1) for i in range(tile_rows // 2))
            gap_even = sum(bf(gap == 2 * i) for i in range(tile_rows // 2))
            span = pl.ds(a * jc, jc)
            moved = None
            for q in range(blocks_full):
                x = pack[c][w, q * size + a * jc:q * size + (a + 1) * jc, :]
                hit = gap == sidef + 2 * q
                full[c][span, lane_block(w, q)] = x * bf(~hit)
                part = x * bf(hit)
                moved = part if moved is None else moved + part
            group = a // (tile_cols // 2)
            inner = a % (tile_cols // 2) * jc
            there, here = lone[inner:inner + jc], swapped[inner:inner + jc]
            to_left, to_right = (there, here) if group == 0 else (here, there)
            moved = moved + to_left * (gap_odd * bf(side == 0)) + to_right * (gap_even * bf(side == 1))
            full[c][span, lane_block(w, blocks_full)] = moved

    fold(0)
    beside = (z > 0).astype(jnp.int32) + (z < n_wide - 1).astype(jnp.int32)
    pl.semaphore_wait(barrier, len(direct) + 1 + beside)

    def h_copy(u, way, s, src):
        ref = pack[u].at[src]
        return pltpu.make_async_remote_copy(
            src_ref=ref, dst_ref=ref, send_sem=h_send.at[u, way, s], recv_sem=h_recv.at[u, way, s],
            device_id=at(z + 1 if way == 0 else z - 1, n), device_id_type=MESH)

    def source(way, s):
        return z - s if way == 0 else z + s

    def has_next(way):
        return z < n_wide - 1 if way == 0 else z > 0

    def has_source(way, s):
        return z >= s if way == 0 else z < n_wide - s

    def h_own(u):
        for way in range(2):
            @pl.when(has_next(way))
            def _():
                h_copy(u, way, 0, z).start()

    def h_pass(u, s):
        for way in range(2):
            @pl.when(has_source(way, s) & has_next(way))
            def _():
                h_copy(u, way, s - 1, source(way, s)).wait_recv()
                h_copy(u, way, s, source(way, s)).start()

    def h_keep(u, s):
        for way in range(2):
            @pl.when(has_source(way, s) & (z == (n_wide - 1 if way == 0 else 0)))
            def _():
                h_copy(u, way, s - 1, source(way, s)).wait_recv()

    def slot(g, c, h):
        return kbuf.at[pl.ds(pl.multiple_of((xor(chip, g, chips) * 2 + c) * kcols + h * hh, hh), hh)]

    def k_copy(g, h, held, to):
        ref = slot(held, core, h)
        return pltpu.make_async_remote_copy(
            src_ref=ref, dst_ref=ref, send_sem=k_send.at[g, h], recv_sem=k_recv.at[g, h],
            device_id=chip_at(to), device_id_type=MESH)

    def k_sent(g, h):
        return k_copy(g, h, 1 + h, 2 - h) if tree and g == 3 else k_copy(g, h, 0, g)

    def sib_copy(g, h, c):
        ref = slot(g, c, h)
        return pltpu.make_async_remote_copy(
            src_ref=ref, dst_ref=ref, send_sem=s_send.at[g, h], recv_sem=s_recv.at[g, h],
            device_id=at(z, chip * 2 + 1 - core), device_id_type=MESH)

    def k_arrive(g, h):
        k_copy(g, h, g, 1).wait_recv()
        if tree and g == 1 + h:
            k_sent(3, h).start()
        sib_copy(g, h, core).start()

    h_own(0)
    fold(1)
    h_own(1)
    tables[1].wait()
    load_k.wait()
    for b in range(tile_rows):
        k_in[tile_span(b), :] = k_in[tile_span(b), :] * mask_rows(ktiles, b, kcols)
    unit = lax.broadcasted_iota(jnp.int32, (kcols, kcols), 0) == lax.broadcasted_iota(jnp.int32, (kcols, kcols), 1)
    kbuf[pl.ds(pl.multiple_of(n * kcols, kcols), kcols), :] = turn(bf(unit), k_in[...])
    order = ((1, 0), (2, 1), (1, 1), (2, 0)) if tree else tuple((g, h) for g in direct for h in range(2))
    for g, h in order:
        k_sent(g, h).start()
    for h in range(2):
        sib_copy(0, h, core).start()
    fold(2)
    for c in range(3):
        fill_own(c)

    h_own(2)
    h_pass(0, 1)
    for g, h in order[:2]:
        k_arrive(g, h)
    h_pass(1, 1)
    for g, h in order[2:]:
        k_arrive(g, h)
    for s in range(2, n_wide - 1):
        h_pass(0, s)
    h_pass(2, 1)
    for s in range(2, n_wide - 1):
        h_pass(1, s)
    if tree:
        for h in range(2):
            k_arrive(3, h)
    for s in range(2, n_wide - 1):
        h_pass(2, s)

    first_near = z // (n_wide - 1)
    far = (n_wide - 1) * (1 - first_near)

    def product(c, w, count):
        span = pl.ds(pl.multiple_of(w * hrows, hrows), count * hrows)
        return jnp.dot(full[c][:, span], kbuf[span, :], preferred_element_type=jnp.float32)

    def ready(c):
        for s in range(1, n_wide - 1):
            h_keep(c, s)

        def step(w, carry):
            @pl.when(w != z)
            def _():
                unfold(c, w)

            return carry

        lax.fori_loop(first_near, first_near + n_wide - 1, step, 0)

    lane = lax.broadcasted_iota(jnp.int32, (1, lanes), 1)
    low = lane < tile

    def finish(c):
        jc, j0 = sizes[c], firsts[c]
        size = tile_cols * jc
        for b2 in range(tile_rows // 2):
            x = acc[:size, lanes * b2:lanes * (b2 + 1)].astype(jnp.bfloat16).astype(jnp.float32)
            y = pltpu.roll(x, tile, 1)
            for odd in range(2):
                both = jnp.where(low, x, y) if odd == 0 else jnp.where(low, y, x)
                for a in range(tile_cols):
                    table[(2 * b2 + odd) * tile_cols + a, :jc] = both[a * jc:(a + 1) * jc]

        def place(t):
            c0, c1 = cols[2 * t], cols[2 * t + 1]
            first = table[rows[2 * t] * tile_cols + c0, :jc]
            second = table[rows[2 * t + 1] * tile_cols + c1, :jc]
            both = jnp.where(low, first, second)
            dest = jnp.where(low, owner[0, c0], owner[0, c1])
            at_lane = pl.ds(t * lanes, lanes)
            for d in range(n_wide):
                lhs[d * jc:(d + 1) * jc, at_lane] = jnp.where(dest == d, both, 0.0).astype(jnp.bfloat16)

        for t in range(pairs // 2):
            place(t)
        blocks = jnp.dot(lhs[:n_wide * jc], phi[...], preferred_element_type=jnp.float32)
        for d in range(n_wide):
            piece = blocks[d * jc:(d + 1) * jc]
            own[d, j0:j0 + jc] = piece
            stage[d, j0:j0 + jc] = piece.astype(jnp.bfloat16)

    def r_copy(c, s):
        span = pl.ds(firsts[c], sizes[c])
        return pltpu.make_async_remote_copy(
            src_ref=stage.at[(z + s) % n_wide, span], dst_ref=landed.at[s - 1, span],
            send_sem=r_send.at[c, s - 1], recv_sem=r_recv.at[c, s - 1],
            device_id=at((z + s) % n_wide, n), device_id_type=MESH)

    def chunk(c):
        size = tile_cols * sizes[c]
        if c > 0:
            ready(c)
        acc[:size] = product(c, first_near, n_wide - 1)
        h_keep(c, n_wide - 1)
        unfold(c, far)
        acc[:size] += product(c, far, 1)
        finish(c)
        for s in range(1, n_wide):
            r_copy(c, s).start()

    ready(0)
    for g in range(chips):
        for h in range(2):
            sib_copy(g, h, 1 - core).wait_recv()
    load_p.wait()
    for load in tables[2:]:
        load.wait()
    for c in range(3):
        chunk(c)

    for c in range(3):
        span = pl.ds(firsts[c], sizes[c])
        total = own[z, span, :]
        for s in range(1, n_wide):
            r_copy(c, s).wait_recv()
            total = total + landed[s - 1, span, :].astype(jnp.float32)
        out_ref[0, span, :] = total

    for c in range(3):
        for s in range(1, n_wide):
            r_copy(c, s).wait_send()
    for g in range(1, chips):
        for h in range(2):
            k_sent(g, h).wait_send()
    for g in range(chips):
        for h in range(2):
            sib_copy(g, h, core).wait_send()
    for u in range(3):
        for way in range(2):
            for s in range(n_wide - 1):
                @pl.when(has_next(way) & has_source(way, s))
                def _():
                    h_copy(u, way, s, source(way, s)).wait_send()


def body(n_wide, n_narrow, kernel, hamiltonian, kernel_tiles, ham_tiles, pair_row, pair_col, sphere_phi, owner):
    pairs, tile, pts = sphere_phi.shape
    height, kcols = kernel.shape
    hrows, breadth = hamiltonian.shape
    tile_rows, tile_cols = ham_tiles.shape
    chips = n_narrow // 2
    hbm = pl.BlockSpec(memory_space=pltpu.HBM)
    dma = pltpu.SemaphoreType.DMA
    sizes = chunk_sizes(tile)
    top = max(sizes)
    bf16 = jnp.bfloat16

    def packed(c):
        size = tile_cols * sizes[c]
        return (tile_rows // 2 - 1) * size + size // 2 + (16 if c == 0 else 0)

    return pl.pallas_call(
        functools.partial(kernel_body, n_wide, n_narrow, tile),
        out_shape=jax.ShapeDtypeStruct((1, tile, pts), jnp.float32),
        in_specs=[hbm] * 8,
        out_specs=pl.BlockSpec(memory_space=pltpu.VMEM),
        scratch_shapes=[
            pltpu.SMEM((tile_cols, tile_rows), jnp.int32),
            pltpu.SMEM((tile_cols, tile_rows), jnp.int32),
            pltpu.SMEM((pairs,), jnp.int32),
            pltpu.SMEM((pairs,), jnp.int32),
            pltpu.SMEM((1, tile_cols), jnp.int32),
            pltpu.VMEM((height, kcols), bf16),
            pltpu.VMEM((hrows, breadth), bf16),
            pltpu.VMEM((hrows, breadth), bf16),
            pltpu.VMEM((pairs * tile, pts), bf16),
            pltpu.VMEM((n_narrow * kcols, height), bf16),
            *[pltpu.VMEM((tile_cols * size, n_wide * hrows), bf16) for size in sizes],
            *[pltpu.VMEM((n_wide, packed(c), 2 * tile), bf16) for c in range(len(sizes))],
            pltpu.VMEM((tile_cols * top, height), jnp.float32),
            pltpu.VMEM((tile_rows * tile_cols, top, 2 * tile), jnp.float32),
            pltpu.VMEM((n_wide * top, pairs * tile), bf16),
            pltpu.VMEM((n_wide, tile, pts), jnp.float32),
            pltpu.VMEM((n_wide, tile, pts), bf16),
            pltpu.VMEM((n_wide - 1, tile, pts), bf16),
            dma((8,)),
            dma((chips, 2)), dma((chips, 2)),
            dma((chips, 2)), dma((chips, 2)),
            dma((3, 2, n_wide)), dma((3, 2, n_wide)),
            dma((3, n_wide)), dma((3, n_wide)),
        ],
        compiler_params=pltpu.CompilerParams(
            collective_id=0, has_side_effects=True, vmem_limit_bytes=60 * 2**20),
    )(kernel_tiles.T, ham_tiles.T, pair_row, pair_col, owner, kernel, hamiltonian,
      sphere_phi.reshape(pairs * tile, pts))


def solution(mesh):
    return jax.shard_map(
        functools.partial(body, mesh.shape["wide"], mesh.shape["narrow"]),
        mesh=mesh,
        in_specs=(
            P("wide", "narrow"),
            P("wide", "narrow"),
            P("wide", "narrow"),
            P("wide", "narrow"),
            P(("wide", "narrow")),
            P(("wide", "narrow")),
            P(("wide", "narrow"), None, None),
            P("narrow", None),
        ),
        out_specs=P(("wide", "narrow"), None, None),
        check_vma=False,
    )
```

```python
import functools

import jax
import jax.numpy as jnp
from jax import lax
from jax.experimental import pallas as pl
from jax.experimental.pallas import tpu as pltpu
from jax.sharding import PartitionSpec as P

MESH = pl.DeviceIdType.MESH
NT = (((1,), (1,)), ((), ()))


NOTE = 16


def xor(a, b, size):
    total, bit = 0, 1
    while bit < size:
        total = total + ((a // bit + b // bit) % 2) * bit
        bit *= 2
    return total


def kernel_body(
    n_wide, n_narrow, tile,
    ktiles_hbm, htiles_hbm, rows_hbm, cols_hbm, owner_hbm, k_hbm, h_hbm, phi_hbm, out_ref,
    ktiles, htiles, rows, cols, owner, k_in, h_in, h_fit, phi, kbuf, full, pack,
    acc, table, lhs, own, stage, landed,
    in_sem, k_send, k_recv, s_send, s_recv, h_send, h_recv, r_send, r_recv,
):
    z = lax.axis_index("wide")
    n = lax.axis_index("narrow")
    chips = n_narrow // 2
    chip, core = n // 2, n % 2
    tile_cols, tile_rows = htiles.shape
    height, kcols = k_hbm.shape
    hrows, breadth = h_hbm.shape
    per = hrows // kcols
    pairs = rows.shape[0]
    lanes = 2 * tile
    blocks_full = tile_rows // 2 - 1
    short = tile // 2
    unit_rows = blocks_full * tile + short
    end_note = NOTE + n_wide * unit_rows
    tree = chips == 4
    hh = kcols // 2

    barrier = pltpu.get_barrier_semaphore()

    def at(w, m):
        return (w, m)

    def chip_at(g):
        return at(z, xor(chip, g, chips) * 2 + core)

    direct = (1, 2) if tree else tuple(range(1, chips))
    for g in direct:
        pl.semaphore_signal(barrier, inc=1, device_id=chip_at(g), device_id_type=MESH)
    pl.semaphore_signal(barrier, inc=1, device_id=at(z, chip * 2 + 1 - core), device_id_type=MESH)
    for way in range(2):
        @pl.when(z < n_wide - 1 if way == 0 else z > 0)
        def _():
            pl.semaphore_signal(barrier, inc=1, device_id=at(z + 1 - 2 * way, n), device_id_type=MESH)

    load_h = pltpu.make_async_copy(h_hbm, h_in, in_sem.at[0])
    load_k = pltpu.make_async_copy(k_hbm, k_in, in_sem.at[1])
    load_p = pltpu.make_async_copy(phi_hbm, phi, in_sem.at[2])
    tables = [
        pltpu.make_async_copy(a, b, in_sem.at[3 + i])
        for i, (a, b) in enumerate((
            (htiles_hbm, htiles), (ktiles_hbm, ktiles), (rows_hbm, rows), (cols_hbm, cols), (owner_hbm, owner)))
    ]
    tables[0].start()
    tables[4].start()
    load_h.start()
    load_k.start()
    for load in tables[1:4]:
        load.start()
    load_p.start()

    def bf(mask):
        return jnp.where(mask, 1.0, 0.0).astype(jnp.bfloat16)

    def spread(values, extent):
        lane_tile = lax.broadcasted_iota(jnp.int32, (1, extent), 1) // tile
        row = jnp.zeros((1, extent), jnp.int32)
        for a in range(tile_cols):
            row = jnp.where(lane_tile == a, values[a], row)
        return row

    def mask_rows(tiles, b, extent):
        return spread([tiles[a, b] for a in range(tile_cols)], extent).astype(jnp.float32).astype(jnp.bfloat16)

    def tile_span(b):
        return pl.ds(b * tile, tile)

    tables[0].wait()
    tables[4].wait()
    holes = []
    for a in range(tile_cols):
        run, count = htiles[a, 0], htiles[a, 0]
        for b in range(1, tile_rows):
            run = run * htiles[a, b]
            count = count + run
        holes.append(count)
    column = [sum(a * (owner[0, a] == d).astype(jnp.int32) for a in range(tile_cols)) for d in range(n_wide)]
    gaps = [sum(holes[a] * (owner[0, a] == d).astype(jnp.int32) for a in range(tile_cols)) for d in range(n_wide)]
    hole = spread(holes, breadth)
    hole_odd = bf(hole % 2 == 1)
    hole_even = bf(hole % 2 == 0)
    lane_half = lax.broadcasted_iota(jnp.int32, (1, breadth), 1) % tile // short
    halves = [bf(lane_half == 0), bf(lane_half == 1)]
    load_h.wait()
    last = []
    for b in (tile_rows - 2, tile_rows - 1):
        h_in[tile_span(b), :] = h_in[tile_span(b), :] * mask_rows(htiles, b, breadth)
        last.append(h_in[tile_span(b), :])
    left_over = last[0] * hole_odd + last[1] * hole_even
    h_fit[tile_span(tile_rows - 2), :] = left_over * halves[0]
    h_fit[tile_span(tile_rows - 1), :] = left_over * halves[1]
    for b in range(tile_rows - 2):
        value = h_in[tile_span(b), :] * mask_rows(htiles, b, breadth)
        h_in[tile_span(b), :] = value
        h_fit[tile_span(b), :] = value + last[b % 2] * bf(hole == b)

    def pick(each):
        r = lax.broadcasted_iota(jnp.int32, (n_wide * each, breadth), 0)
        col = lax.broadcasted_iota(jnp.int32, (n_wide * each, breadth), 1)
        want = r % each
        for d in range(n_wide):
            want = want + jnp.where(r // each == d, column[d] * tile, 0)
        return want, col

    def turn(which, x):
        return lax.dot_general(which, x, NT, preferred_element_type=jnp.float32).astype(jnp.bfloat16)

    want, col = pick(tile)
    choose = bf(col == want)
    out = turn(choose, h_fit[:tile * (tile_rows - 2), :])
    for d in range(n_wide):
        for q in range(blocks_full):
            start = NOTE + d * unit_rows + q * tile
            pack[z, start:start + tile, :] = out[d * tile:(d + 1) * tile, q * lanes:(q + 1) * lanes]
    want, col = pick(short)
    out = turn(bf((col == want) | (col == want + short)), h_fit[tile * (tile_rows - 2):, :])
    for d in range(n_wide):
        start = NOTE + d * unit_rows + blocks_full * tile
        pack[z, start:start + short, :] = out[d * short:(d + 1) * short]
    note_row = lax.broadcasted_iota(jnp.int32, (NOTE, lanes), 0)
    note = jnp.zeros((NOTE, lanes), jnp.int32)
    for d in range(n_wide):
        note = jnp.where(note_row == d, gaps[d], note)
    note = note.astype(jnp.float32).astype(jnp.bfloat16)
    pack[z, :NOTE, :] = note
    pack[z, end_note:, :] = note

    side = lax.broadcasted_iota(jnp.int32, (1, lanes), 1) // tile
    sidef = side.astype(jnp.float32)

    def lane_block(w, q):
        return pl.ds(pl.multiple_of(w * hrows + q * lanes, lanes), lanes)

    def unfold(d, w):
        above = (w > z).astype(jnp.int32)
        notes = pack[w, pl.ds(pl.multiple_of(above * end_note, NOTE), NOTE), :].astype(jnp.float32)
        gap = jnp.sum(jnp.where(note_row == d, notes, 0.0), axis=0, keepdims=True)
        gap_odd = sum(bf(gap == 2 * i + 1) for i in range(tile_rows // 2))
        gap_even = sum(bf(gap == 2 * i) for i in range(tile_rows // 2))
        start = NOTE + d * unit_rows
        lone = pack[w, pl.ds(pl.multiple_of(start + blocks_full * tile, NOTE), short), :]
        swapped = pltpu.roll(lone.astype(jnp.float32), tile, 1).astype(jnp.bfloat16)
        moved = None
        for q in range(blocks_full):
            x = pack[w, pl.ds(pl.multiple_of(start + q * tile, NOTE), tile), :]
            hit = gap == sidef + 2 * q
            full[d, :, lane_block(w, q)] = x * bf(~hit)
            part = x * bf(hit)
            moved = part if moved is None else moved + part
        left = gap_odd * bf(side == 0)
        right = gap_even * bf(side == 1)
        full[d, :short, lane_block(w, blocks_full)] = moved[:short] + lone * left + swapped * right
        full[d, short:, lane_block(w, blocks_full)] = moved[short:] + swapped * left + lone * right

    beside = (z > 0).astype(jnp.int32) + (z < n_wide - 1).astype(jnp.int32)
    pl.semaphore_wait(barrier, len(direct) + 1 + beside)

    def h_copy(u, way, s, src):
        d = u if way == 0 else n_wide - 1 - u
        start, count = NOTE + d * unit_rows, unit_rows
        if u == 0:
            start, count = start - (NOTE if way == 0 else 0), count + NOTE
        ref = pack.at[src, pl.ds(start, count)]
        return pltpu.make_async_remote_copy(
            src_ref=ref, dst_ref=ref, send_sem=h_send.at[u, way, s], recv_sem=h_recv.at[u, way, s],
            device_id=at(z + 1 if way == 0 else z - 1, n), device_id_type=MESH)

    def source(way, s):
        return z - s if way == 0 else z + s

    def has_next(way):
        return z < n_wide - 1 if way == 0 else z > 0

    def has_source(way, s):
        return z >= s if way == 0 else z < n_wide - s

    def h_own(u):
        for way in range(2):
            @pl.when(has_next(way))
            def _():
                h_copy(u, way, 0, z).start()

    def h_pass(u, s):
        for way in range(2):
            @pl.when(has_source(way, s) & has_next(way))
            def _():
                h_copy(u, way, s - 1, source(way, s)).wait_recv()
                h_copy(u, way, s, source(way, s)).start()

    def h_keep(u, s):
        for way in range(2):
            @pl.when(has_source(way, s) & (z == (n_wide - 1 if way == 0 else 0)))
            def _():
                h_copy(u, way, s - 1, source(way, s)).wait_recv()

    def slot(g, c, h):
        return kbuf.at[pl.ds(pl.multiple_of((xor(chip, g, chips) * 2 + c) * kcols + h * hh, hh), hh)]

    def k_copy(g, h, held, to):
        ref = slot(held, core, h)
        return pltpu.make_async_remote_copy(
            src_ref=ref, dst_ref=ref, send_sem=k_send.at[g, h], recv_sem=k_recv.at[g, h],
            device_id=chip_at(to), device_id_type=MESH)

    def k_sent(g, h):
        return k_copy(g, h, 1 + h, 2 - h) if tree and g == 3 else k_copy(g, h, 0, g)

    def sib_copy(g, h, c):
        ref = slot(g, c, h)
        return pltpu.make_async_remote_copy(
            src_ref=ref, dst_ref=ref, send_sem=s_send.at[g, h], recv_sem=s_recv.at[g, h],
            device_id=at(z, chip * 2 + 1 - core), device_id_type=MESH)

    def k_arrive(g, h):
        k_copy(g, h, g, 1).wait_recv()
        if tree and g == 1 + h:
            k_sent(3, h).start()
        sib_copy(g, h, core).start()

    h_own(0)
    h_own(1)
    tables[1].wait()
    load_k.wait()
    for b in range(tile_rows):
        k_in[tile_span(b), :] = k_in[tile_span(b), :] * mask_rows(ktiles, b, kcols)
    unit = lax.broadcasted_iota(jnp.int32, (kcols, kcols), 0) == lax.broadcasted_iota(jnp.int32, (kcols, kcols), 1)
    kbuf[pl.ds(pl.multiple_of(n * kcols, kcols), kcols), :] = turn(bf(unit), k_in[...])
    order = ((1, 0), (2, 1), (1, 1), (2, 0)) if tree else tuple((g, h) for g in direct for h in range(2))
    for g, h in order:
        k_sent(g, h).start()
    for h in range(2):
        sib_copy(0, h, core).start()
    out = turn(choose, h_in[...])
    for d in range(n_wide):
        full[d, :, pl.ds(pl.multiple_of(z * hrows, hrows), hrows)] = out[d * tile:(d + 1) * tile]

    units = n_wide
    kernel_steps = [order[:2], order[2:]] + ([((3, 0), (3, 1))] if tree else [])
    k_after = [(1, 1), (1, n_wide - 2), (units - 1, n_wide - 2)]
    waits = sorted(((u, s) for u in range(units) for s in range(1, n_wide - 1)), key=lambda us: (us[0] + us[1], us[1]))
    sent = 2
    for u, s in waits:
        h_pass(u, s)
        if sent < units and u + s >= sent:
            h_own(sent)
            sent += 1
        if (u, s) in k_after and kernel_steps:
            for g, h in kernel_steps.pop(0):
                k_arrive(g, h)
    for u in range(sent, units):
        h_own(u)
    for steps in kernel_steps:
        for g, h in steps:
            k_arrive(g, h)

    first_near = z // (n_wide - 1)
    far = (n_wide - 1) * (1 - first_near)

    upper = z // (n_wide // 2)
    lane = lax.broadcasted_iota(jnp.int32, (1, lanes), 1)
    low = lane < tile

    def target(i):
        if i == n_wide - 1:
            return z
        down = n_wide - 1 - i
        return upper * (i + (i >= z).astype(jnp.int32)) + (1 - upper) * (down - (down <= z).astype(jnp.int32))

    def product(d, w, count):
        span = pl.ds(pl.multiple_of(w * hrows, hrows), count * hrows)
        return jnp.dot(full[d, :, span], kbuf[span, :], preferred_element_type=jnp.float32)

    def ready(i):
        for s in range(1, n_wide - 1):
            h_keep(i, s)

        def step(w, carry):
            @pl.when(w != z)
            def _():
                unfold(target(i), w)

            return carry

        lax.fori_loop(first_near, first_near + n_wide - 1, step, 0)

    def r_copy(i):
        d = target(i)
        return pltpu.make_async_remote_copy(
            src_ref=stage.at[i], dst_ref=landed.at[z], send_sem=r_send.at[i], recv_sem=r_recv.at[z],
            device_id=at(d, n), device_id_type=MESH)

    def r_wait(s):
        src = (z + s) % n_wide
        pltpu.make_async_remote_copy(
            src_ref=stage.at[0], dst_ref=landed.at[src], send_sem=r_send.at[0], recv_sem=r_recv.at[src],
            device_id=at(src, n), device_id_type=MESH).wait_recv()

    def finish(i):
        d = target(i)
        for b2 in range(tile_rows // 2):
            x = acc[:, lanes * b2:lanes * (b2 + 1)]
            y = pltpu.roll(x, tile, 1)
            table[2 * b2] = jnp.where(low, x, y).astype(jnp.bfloat16)
            table[2 * b2 + 1] = jnp.where(low, y, x).astype(jnp.bfloat16)
        for t in range(pairs // 2):
            kept = [(owner[0, cols[2 * t + k]] == d).astype(jnp.int32) for k in range(2)]
            left = jnp.where(low, kept[0], 0).astype(jnp.float32).astype(jnp.bfloat16)
            right = jnp.where(low, 0, kept[1]).astype(jnp.float32).astype(jnp.bfloat16)
            lhs[:, t * lanes:(t + 1) * lanes] = table[rows[2 * t]] * left + table[rows[2 * t + 1]] * right
        return jnp.dot(lhs[...], phi[...], preferred_element_type=jnp.float32)

    def chunk(i):
        if i > 1:
            ready(i)
        d = target(i)
        acc[...] = product(d, first_near, n_wide - 1)
        h_keep(i, n_wide - 1)
        unfold(d, far)
        acc[...] += product(d, far, 1)
        block = finish(i)
        if i < n_wide - 1:
            stage[i] = block.astype(jnp.bfloat16)
            r_copy(i).start()
        else:
            own[...] = block

    ready(0)
    ready(1)
    for g in range(chips):
        for h in range(2):
            sib_copy(g, h, 1 - core).wait_recv()
    load_p.wait()
    for load in tables[2:4]:
        load.wait()
    for i in range(n_wide):
        chunk(i)

    total = own[...]
    for s in range(1, n_wide):
        r_wait(s)
        total = total + landed[(z + s) % n_wide].astype(jnp.float32)
    out_ref[0] = total

    for i in range(n_wide - 1):
        r_copy(i).wait_send()
    for g in range(1, chips):
        for h in range(2):
            k_sent(g, h).wait_send()
    for g in range(chips):
        for h in range(2):
            sib_copy(g, h, core).wait_send()
    for u in range(n_wide):
        for way in range(2):
            for s in range(n_wide - 1):
                @pl.when(has_next(way) & has_source(way, s))
                def _():
                    h_copy(u, way, s, source(way, s)).wait_send()


def body(n_wide, n_narrow, kernel, hamiltonian, kernel_tiles, ham_tiles, pair_row, pair_col, sphere_phi, owner):
    pairs, tile, pts = sphere_phi.shape
    height, kcols = kernel.shape
    hrows, breadth = hamiltonian.shape
    tile_rows, tile_cols = ham_tiles.shape
    chips = n_narrow // 2
    hbm = pl.BlockSpec(memory_space=pltpu.HBM)
    dma = pltpu.SemaphoreType.DMA
    unit_rows = (tile_rows // 2 - 1) * tile + tile // 2
    bf16 = jnp.bfloat16

    return pl.pallas_call(
        functools.partial(kernel_body, n_wide, n_narrow, tile),
        out_shape=jax.ShapeDtypeStruct((1, tile, pts), jnp.float32),
        in_specs=[hbm] * 8,
        out_specs=pl.BlockSpec(memory_space=pltpu.VMEM),
        scratch_shapes=[
            pltpu.SMEM((tile_cols, tile_rows), jnp.int32),
            pltpu.SMEM((tile_cols, tile_rows), jnp.int32),
            pltpu.SMEM((pairs,), jnp.int32),
            pltpu.SMEM((pairs,), jnp.int32),
            pltpu.SMEM((1, tile_cols), jnp.int32),
            pltpu.VMEM((height, kcols), bf16),
            pltpu.VMEM((hrows, breadth), bf16),
            pltpu.VMEM((hrows, breadth), bf16),
            pltpu.VMEM((pairs * tile, pts), bf16),
            pltpu.VMEM((n_narrow * kcols, height), bf16),
            pltpu.VMEM((n_wide, tile, n_wide * hrows), bf16),
            pltpu.VMEM((n_wide, n_wide * unit_rows + 2 * NOTE, 2 * tile), bf16),
            pltpu.VMEM((tile, height), jnp.float32),
            pltpu.VMEM((tile_rows, tile, 2 * tile), bf16),
            pltpu.VMEM((tile, pairs * tile), bf16),
            pltpu.VMEM((tile, pts), jnp.float32),
            pltpu.VMEM((n_wide - 1, tile, pts), bf16),
            pltpu.VMEM((n_wide, tile, pts), bf16),
            dma((8,)),
            dma((chips, 2)), dma((chips, 2)),
            dma((chips, 2)), dma((chips, 2)),
            dma((n_wide, 2, n_wide)), dma((n_wide, 2, n_wide)),
            dma((n_wide,)), dma((n_wide,)),
        ],
        compiler_params=pltpu.CompilerParams(
            collective_id=0, has_side_effects=True, vmem_limit_bytes=60 * 2**20),
    )(kernel_tiles.T, ham_tiles.T, pair_row, pair_col, owner, kernel, hamiltonian,
      sphere_phi.reshape(pairs * tile, pts))


def solution(mesh):
    return jax.shard_map(
        functools.partial(body, mesh.shape["wide"], mesh.shape["narrow"]),
        mesh=mesh,
        in_specs=(
            P("wide", "narrow"),
            P("wide", "narrow"),
            P("wide", "narrow"),
            P("wide", "narrow"),
            P(("wide", "narrow")),
            P(("wide", "narrow")),
            P(("wide", "narrow"), None, None),
            P("narrow", None),
        ),
        out_specs=P(("wide", "narrow"), None, None),
        check_vma=False,
    )
```

```python
import functools

import jax
import jax.numpy as jnp
from jax import lax
from jax.experimental import pallas as pl
from jax.experimental.pallas import tpu as pltpu
from jax.sharding import PartitionSpec as P

MESH = pl.DeviceIdType.MESH
NT = (((1,), (1,)), ((), ()))


NOTE = 16


def xor(a, b, size):
    total, bit = 0, 1
    while bit < size:
        total = total + ((a // bit + b // bit) % 2) * bit
        bit *= 2
    return total


def kernel_body(
    n_wide, n_narrow, tile,
    ktiles_hbm, htiles_hbm, rows_hbm, cols_hbm, owner_hbm, k_hbm, h_hbm, phi_hbm, out_ref,
    ktiles, htiles, rows, cols, owner, k_in, h_in, h_fit, phi, kbuf, full, pack,
    acc, table, lhs, own, stage, landed,
    in_sem, k_send, k_recv, s_send, s_recv, h_send, h_recv, r_send, r_recv,
):
    z = lax.axis_index("wide")
    n = lax.axis_index("narrow")
    chips = n_narrow // 2
    chip, core = n // 2, n % 2
    tile_cols, tile_rows = htiles.shape
    height, kcols = k_hbm.shape
    hrows, breadth = h_hbm.shape
    per = hrows // kcols
    pairs = rows.shape[0]
    lanes = 2 * tile
    blocks_full = tile_rows // 2 - 1
    short = tile // 2
    unit_rows = blocks_full * tile + short
    end_note = NOTE + n_wide * unit_rows
    groups = n_wide // 2
    tree = chips == 4
    hh = kcols // 2

    barrier = pltpu.get_barrier_semaphore()

    def at(w, m):
        return (w, m)

    def chip_at(g):
        return at(z, xor(chip, g, chips) * 2 + core)

    direct = (1, 2) if tree else tuple(range(1, chips))
    for g in direct:
        pl.semaphore_signal(barrier, inc=1, device_id=chip_at(g), device_id_type=MESH)
    pl.semaphore_signal(barrier, inc=1, device_id=at(z, chip * 2 + 1 - core), device_id_type=MESH)
    for way in range(2):
        @pl.when(z < n_wide - 1 if way == 0 else z > 0)
        def _():
            pl.semaphore_signal(barrier, inc=1, device_id=at(z + 1 - 2 * way, n), device_id_type=MESH)

    load_h = pltpu.make_async_copy(h_hbm, h_in, in_sem.at[0])
    load_k = pltpu.make_async_copy(k_hbm, k_in, in_sem.at[1])
    load_p = pltpu.make_async_copy(phi_hbm, phi, in_sem.at[2])
    tables = [
        pltpu.make_async_copy(a, b, in_sem.at[3 + i])
        for i, (a, b) in enumerate((
            (htiles_hbm, htiles), (ktiles_hbm, ktiles), (rows_hbm, rows), (cols_hbm, cols), (owner_hbm, owner)))
    ]
    tables[0].start()
    tables[4].start()
    load_h.start()
    load_k.start()
    for load in tables[1:4]:
        load.start()
    load_p.start()

    def bf(mask):
        return jnp.where(mask, 1.0, 0.0).astype(jnp.bfloat16)

    def spread(values, extent):
        lane_tile = lax.broadcasted_iota(jnp.int32, (1, extent), 1) // tile
        row = jnp.zeros((1, extent), jnp.int32)
        for a in range(tile_cols):
            row = jnp.where(lane_tile == a, values[a], row)
        return row

    def mask_rows(tiles, b, extent):
        return spread([tiles[a, b] for a in range(tile_cols)], extent).astype(jnp.float32).astype(jnp.bfloat16)

    def tile_span(b):
        return pl.ds(b * tile, tile)

    tables[0].wait()
    tables[4].wait()
    holes = []
    for a in range(tile_cols):
        run, count = htiles[a, 0], htiles[a, 0]
        for b in range(1, tile_rows):
            run = run * htiles[a, b]
            count = count + run
        holes.append(count)
    column = [sum(a * (owner[0, a] == d).astype(jnp.int32) for a in range(tile_cols)) for d in range(n_wide)]
    gaps = [sum(holes[a] * (owner[0, a] == d).astype(jnp.int32) for a in range(tile_cols)) for d in range(n_wide)]
    hole = spread(holes, breadth)
    hole_odd = bf(hole % 2 == 1)
    hole_even = bf(hole % 2 == 0)
    lane_half = lax.broadcasted_iota(jnp.int32, (1, breadth), 1) % tile // short
    halves = [bf(lane_half == 0), bf(lane_half == 1)]
    load_h.wait()
    last = []
    for b in (tile_rows - 2, tile_rows - 1):
        h_in[tile_span(b), :] = h_in[tile_span(b), :] * mask_rows(htiles, b, breadth)
        last.append(h_in[tile_span(b), :])
    left_over = last[0] * hole_odd + last[1] * hole_even
    h_fit[tile_span(tile_rows - 2), :] = left_over * halves[0]
    h_fit[tile_span(tile_rows - 1), :] = left_over * halves[1]
    for b in range(tile_rows - 2):
        value = h_in[tile_span(b), :] * mask_rows(htiles, b, breadth)
        h_in[tile_span(b), :] = value
        h_fit[tile_span(b), :] = value + last[b % 2] * bf(hole == b)

    def pick(each):
        r = lax.broadcasted_iota(jnp.int32, (n_wide * each, breadth), 0)
        col = lax.broadcasted_iota(jnp.int32, (n_wide * each, breadth), 1)
        want = r % each
        for d in range(n_wide):
            want = want + jnp.where(r // each == d, column[d] * tile, 0)
        return want, col

    def turn(which, x):
        return lax.dot_general(which, x, NT, preferred_element_type=jnp.float32).astype(jnp.bfloat16)

    want, col = pick(tile)
    choose = bf(col == want)
    out = turn(choose, h_fit[:tile * (tile_rows - 2), :])
    for d in range(n_wide):
        for q in range(blocks_full):
            start = NOTE + d * unit_rows + q * tile
            pack[z, start:start + tile, :] = out[d * tile:(d + 1) * tile, q * lanes:(q + 1) * lanes]
    want, col = pick(short)
    out = turn(bf((col == want) | (col == want + short)), h_fit[tile * (tile_rows - 2):, :])
    for d in range(n_wide):
        start = NOTE + d * unit_rows + blocks_full * tile
        pack[z, start:start + short, :] = out[d * short:(d + 1) * short]
    note_row = lax.broadcasted_iota(jnp.int32, (NOTE, lanes), 0)
    note = jnp.zeros((NOTE, lanes), jnp.int32)
    for d in range(n_wide):
        note = jnp.where(note_row == d, gaps[d], note)
    note = note.astype(jnp.float32).astype(jnp.bfloat16)
    pack[z, :NOTE, :] = note
    pack[z, end_note:, :] = note

    side = lax.broadcasted_iota(jnp.int32, (1, lanes), 1) // tile
    sidef = side.astype(jnp.float32)

    def lane_block(w, q):
        return pl.ds(pl.multiple_of(w * hrows + q * lanes, lanes), lanes)

    def unfold(g, w):
        above = (w > z).astype(jnp.int32)
        notes = pack[w, pl.ds(pl.multiple_of(above * end_note, NOTE), NOTE), :].astype(jnp.float32)
        for k in range(2):
            gap = jnp.sum(jnp.where(note_row == 2 * g + k, notes, 0.0), axis=0, keepdims=True)
            gap_odd = sum(bf(gap == 2 * i + 1) for i in range(tile_rows // 2))
            gap_even = sum(bf(gap == 2 * i) for i in range(tile_rows // 2))
            start = NOTE + (2 * g + k) * unit_rows
            lone = pack[w, pl.ds(pl.multiple_of(start + blocks_full * tile, NOTE), short), :]
            swapped = pltpu.roll(lone.astype(jnp.float32), tile, 1).astype(jnp.bfloat16)
            moved = None
            top = k * tile
            for q in range(blocks_full):
                x = pack[w, pl.ds(pl.multiple_of(start + q * tile, NOTE), tile), :]
                hit = gap == sidef + 2 * q
                full[g, top:top + tile, lane_block(w, q)] = x * bf(~hit)
                part = x * bf(hit)
                moved = part if moved is None else moved + part
            left = gap_odd * bf(side == 0)
            right = gap_even * bf(side == 1)
            half = top + short
            full[g, top:half, lane_block(w, blocks_full)] = moved[:short] + lone * left + swapped * right
            full[g, half:top + tile, lane_block(w, blocks_full)] = moved[short:] + swapped * left + lone * right

    beside = (z > 0).astype(jnp.int32) + (z < n_wide - 1).astype(jnp.int32)
    pl.semaphore_wait(barrier, len(direct) + 1 + beside)

    def h_copy(u, way, s, src):
        if u == 0:
            start, count = 0 if way == 0 else NOTE + (n_wide - 2) * unit_rows, NOTE + 2 * unit_rows
        else:
            start, count = NOTE + (u + 1 if way == 0 else n_wide - 2 - u) * unit_rows, unit_rows
        ref = pack.at[src, pl.ds(start, count)]
        return pltpu.make_async_remote_copy(
            src_ref=ref, dst_ref=ref, send_sem=h_send.at[u, way, s], recv_sem=h_recv.at[u, way, s],
            device_id=at(z + 1 if way == 0 else z - 1, n), device_id_type=MESH)

    def source(way, s):
        return z - s if way == 0 else z + s

    def has_next(way):
        return z < n_wide - 1 if way == 0 else z > 0

    def has_source(way, s):
        return z >= s if way == 0 else z < n_wide - s

    def h_own(u):
        for way in range(2):
            @pl.when(has_next(way))
            def _():
                h_copy(u, way, 0, z).start()

    def h_pass(u, s):
        for way in range(2):
            @pl.when(has_source(way, s) & has_next(way))
            def _():
                h_copy(u, way, s - 1, source(way, s)).wait_recv()
                h_copy(u, way, s, source(way, s)).start()

    def h_keep(u, s):
        for way in range(2):
            @pl.when(has_source(way, s) & (z == (n_wide - 1 if way == 0 else 0)))
            def _():
                h_copy(u, way, s - 1, source(way, s)).wait_recv()

    def slot(g, c, h):
        return kbuf.at[pl.ds(pl.multiple_of((xor(chip, g, chips) * 2 + c) * kcols + h * hh, hh), hh)]

    def k_copy(g, h, held, to):
        ref = slot(held, core, h)
        return pltpu.make_async_remote_copy(
            src_ref=ref, dst_ref=ref, send_sem=k_send.at[g, h], recv_sem=k_recv.at[g, h],
            device_id=chip_at(to), device_id_type=MESH)

    def k_sent(g, h):
        return k_copy(g, h, 1 + h, 2 - h) if tree and g == 3 else k_copy(g, h, 0, g)

    def sib_copy(g, h, c):
        ref = slot(g, c, h)
        return pltpu.make_async_remote_copy(
            src_ref=ref, dst_ref=ref, send_sem=s_send.at[g, h], recv_sem=s_recv.at[g, h],
            device_id=at(z, chip * 2 + 1 - core), device_id_type=MESH)

    def k_arrive(g, h):
        k_copy(g, h, g, 1).wait_recv()
        if tree and g == 1 + h:
            k_sent(3, h).start()
        sib_copy(g, h, core).start()

    for u in range(n_wide - 1):
        h_own(u)
    tables[1].wait()
    load_k.wait()
    for b in range(tile_rows):
        k_in[tile_span(b), :] = k_in[tile_span(b), :] * mask_rows(ktiles, b, kcols)
    unit = lax.broadcasted_iota(jnp.int32, (kcols, kcols), 0) == lax.broadcasted_iota(jnp.int32, (kcols, kcols), 1)
    kbuf[pl.ds(pl.multiple_of(n * kcols, kcols), kcols), :] = turn(bf(unit), k_in[...])
    order = ((1, 0), (2, 1), (1, 1), (2, 0)) if tree else tuple((g, h) for g in direct for h in range(2))
    for g, h in order:
        k_sent(g, h).start()
    for h in range(2):
        sib_copy(0, h, core).start()
    out = turn(choose, h_in[...])
    for g in range(groups):
        full[g, :, pl.ds(pl.multiple_of(z * hrows, hrows), hrows)] = out[2 * g * tile:2 * (g + 1) * tile]

    kernel_steps = [order[:2], order[2:]] + ([((3, 0), (3, 1))] if tree else [])
    for s in range(1, n_wide - 1):
        for u in range(n_wide - 1):
            h_pass(u, s)
            if kernel_steps and (u, s) in ((0, 1), (1, 1), (0, 2)):
                for g, h in kernel_steps.pop(0):
                    k_arrive(g, h)
    for steps in kernel_steps:
        for g, h in steps:
            k_arrive(g, h)

    first_near = z // (n_wide - 1)
    far = (n_wide - 1) * (1 - first_near)

    upper = z // (n_wide // 2)
    lane = lax.broadcasted_iota(jnp.int32, (1, lanes), 1)
    low = lane < tile

    def group(i):
        return upper * i + (1 - upper) * (groups - 1 - i)

    def product(g, w, count):
        span = pl.ds(pl.multiple_of(w * hrows, hrows), count * hrows)
        return jnp.dot(full[g, :, span], kbuf[span, :], preferred_element_type=jnp.float32)

    def keeps(i):
        return (0,) if i == 0 else (2 * i - 1, 2 * i)

    def ready(i):
        for u in keeps(i):
            for s in range(1, n_wide - 1):
                h_keep(u, s)

        def step(w, carry):
            @pl.when(w != z)
            def _():
                unfold(group(i), w)

            return carry

        lax.fori_loop(first_near, first_near + n_wide - 1, step, 0)

    def r_copy(i, k):
        return pltpu.make_async_remote_copy(
            src_ref=stage.at[2 * i + k], dst_ref=landed.at[z], send_sem=r_send.at[2 * i + k], recv_sem=r_recv.at[z],
            device_id=at(2 * group(i) + k, n), device_id_type=MESH)

    def r_wait(s):
        src = (z + s) % n_wide
        pltpu.make_async_remote_copy(
            src_ref=stage.at[0], dst_ref=landed.at[src], send_sem=r_send.at[0], recv_sem=r_recv.at[src],
            device_id=at(src, n), device_id_type=MESH).wait_recv()

    def finish(i):
        g = group(i)
        for b2 in range(tile_rows // 2):
            x = acc[:, lanes * b2:lanes * (b2 + 1)]
            y = pltpu.roll(x, tile, 1)
            table[2 * b2] = jnp.where(low, x, y).astype(jnp.bfloat16)
            table[2 * b2 + 1] = jnp.where(low, y, x).astype(jnp.bfloat16)

        def place(t, carry):
            to = [owner[0, cols[2 * t + side]] for side in range(2)]
            at_lane = pl.ds(pl.multiple_of(t * lanes, lanes), lanes)
            for k in range(2):
                kept = [(one == 2 * g + k).astype(jnp.int32) for one in to]
                left = jnp.where(low, kept[0], 0).astype(jnp.float32).astype(jnp.bfloat16)
                right = jnp.where(low, 0, kept[1]).astype(jnp.float32).astype(jnp.bfloat16)
                span = pl.ds(k * tile, tile)
                lhs[span, at_lane] = table[rows[2 * t], span] * left + table[rows[2 * t + 1], span] * right
            return carry

        lax.fori_loop(0, pairs // 2, place, 0, unroll=4)
        return jnp.dot(lhs[...], phi[...], preferred_element_type=jnp.float32)

    def chunk(i):
        if i > 0:
            ready(i)
        g = group(i)
        acc[...] = product(g, first_near, n_wide - 1)
        for u in keeps(i):
            h_keep(u, n_wide - 1)
        unfold(g, far)
        acc[...] += product(g, far, 1)
        blocks = finish(i)
        for k in range(2):
            block = blocks[k * tile:(k + 1) * tile]

            @pl.when(2 * g + k == z)
            def _():
                own[...] = block

            @pl.when(2 * g + k != z)
            def _():
                stage[2 * i + k] = block.astype(jnp.bfloat16)
                r_copy(i, k).start()

    ready(0)
    for g in range(chips):
        for h in range(2):
            sib_copy(g, h, 1 - core).wait_recv()
    load_p.wait()
    for load in tables[2:4]:
        load.wait()
    for i in range(groups):
        chunk(i)

    total = own[...]
    for s in range(1, n_wide):
        r_wait(s)
        total = total + landed[(z + s) % n_wide].astype(jnp.float32)
    out_ref[0] = total

    for i in range(groups):
        for k in range(2):
            @pl.when(2 * group(i) + k != z)
            def _():
                r_copy(i, k).wait_send()
    for g in range(1, chips):
        for h in range(2):
            k_sent(g, h).wait_send()
    for g in range(chips):
        for h in range(2):
            sib_copy(g, h, core).wait_send()
    for u in range(n_wide - 1):
        for way in range(2):
            for s in range(n_wide - 1):
                @pl.when(has_next(way) & has_source(way, s))
                def _():
                    h_copy(u, way, s, source(way, s)).wait_send()


def body(n_wide, n_narrow, kernel, hamiltonian, kernel_tiles, ham_tiles, pair_row, pair_col, sphere_phi, owner):
    pairs, tile, pts = sphere_phi.shape
    height, kcols = kernel.shape
    hrows, breadth = hamiltonian.shape
    tile_rows, tile_cols = ham_tiles.shape
    chips = n_narrow // 2
    hbm = pl.BlockSpec(memory_space=pltpu.HBM)
    dma = pltpu.SemaphoreType.DMA
    unit_rows = (tile_rows // 2 - 1) * tile + tile // 2
    bf16 = jnp.bfloat16

    return pl.pallas_call(
        functools.partial(kernel_body, n_wide, n_narrow, tile),
        out_shape=jax.ShapeDtypeStruct((1, tile, pts), jnp.float32),
        in_specs=[hbm] * 8,
        out_specs=pl.BlockSpec(memory_space=pltpu.VMEM),
        scratch_shapes=[
            pltpu.SMEM((tile_cols, tile_rows), jnp.int32),
            pltpu.SMEM((tile_cols, tile_rows), jnp.int32),
            pltpu.SMEM((pairs,), jnp.int32),
            pltpu.SMEM((pairs,), jnp.int32),
            pltpu.SMEM((1, tile_cols), jnp.int32),
            pltpu.VMEM((height, kcols), bf16),
            pltpu.VMEM((hrows, breadth), bf16),
            pltpu.VMEM((hrows, breadth), bf16),
            pltpu.VMEM((pairs * tile, pts), bf16),
            pltpu.VMEM((n_narrow * kcols, height), bf16),
            pltpu.VMEM((n_wide // 2, 2 * tile, n_wide * hrows), bf16),
            pltpu.VMEM((n_wide, n_wide * unit_rows + 2 * NOTE, 2 * tile), bf16),
            pltpu.VMEM((2 * tile, height), jnp.float32),
            pltpu.VMEM((tile_rows, 2 * tile, 2 * tile), bf16),
            pltpu.VMEM((2 * tile, pairs * tile), bf16),
            pltpu.VMEM((tile, pts), jnp.float32),
            pltpu.VMEM((n_wide, tile, pts), bf16),
            pltpu.VMEM((n_wide, tile, pts), bf16),
            dma((8,)),
            dma((chips, 2)), dma((chips, 2)),
            dma((chips, 2)), dma((chips, 2)),
            dma((n_wide, 2, n_wide)), dma((n_wide, 2, n_wide)),
            dma((n_wide,)), dma((n_wide,)),
        ],
        compiler_params=pltpu.CompilerParams(
            collective_id=0, has_side_effects=True, vmem_limit_bytes=60 * 2**20),
    )(kernel_tiles.T, ham_tiles.T, pair_row, pair_col, owner, kernel, hamiltonian,
      sphere_phi.reshape(pairs * tile, pts))


def solution(mesh):
    return jax.shard_map(
        functools.partial(body, mesh.shape["wide"], mesh.shape["narrow"]),
        mesh=mesh,
        in_specs=(
            P("wide", "narrow"),
            P("wide", "narrow"),
            P("wide", "narrow"),
            P("wide", "narrow"),
            P(("wide", "narrow")),
            P(("wide", "narrow")),
            P(("wide", "narrow"), None, None),
            P("narrow", None),
        ),
        out_specs=P(("wide", "narrow"), None, None),
        check_vma=False,
    )
```

```python
import functools

import jax
import jax.numpy as jnp
from jax import lax
from jax.experimental import pallas as pl
from jax.experimental.pallas import tpu as pltpu
from jax.sharding import PartitionSpec as P

MESH = pl.DeviceIdType.MESH
NT = (((1,), (1,)), ((), ()))


NOTE = 16


def xor(a, b, size):
    total, bit = 0, 1
    while bit < size:
        total = total + ((a // bit + b // bit) % 2) * bit
        bit *= 2
    return total


def kernel_body(
    n_wide, n_narrow, tile,
    ktiles_hbm, htiles_hbm, rows_hbm, cols_hbm, owner_hbm, k_hbm, h_hbm, phi_hbm, own_out, landed,
    ktiles, htiles, rows, cols, owner, k_in, h_in, h_fit, phi, kbuf, full, pack,
    acc, table, lhs, own, stage,
    in_sem, own_sem, k_send, k_recv, s_send, s_recv, h_send, h_recv, r_send, r_recv,
):
    z = lax.axis_index("wide")
    n = lax.axis_index("narrow")
    chips = n_narrow // 2
    chip, core = n // 2, n % 2
    tile_cols, tile_rows = htiles.shape
    height, kcols = k_hbm.shape
    hrows, breadth = h_hbm.shape
    per = hrows // kcols
    pairs = rows.shape[0]
    lanes = 2 * tile
    blocks_full = tile_rows // 2 - 1
    short = tile // 2
    unit_rows = blocks_full * tile + short
    end_note = NOTE + n_wide * unit_rows
    groups = n_wide // 2
    tree = chips == 4
    hh = kcols // 2

    barrier = pltpu.get_barrier_semaphore()

    def at(w, m):
        return (w, m)

    def chip_at(g):
        return at(z, xor(chip, g, chips) * 2 + core)

    direct = (1, 2) if tree else tuple(range(1, chips))
    for g in direct:
        pl.semaphore_signal(barrier, inc=1, device_id=chip_at(g), device_id_type=MESH)
    pl.semaphore_signal(barrier, inc=1, device_id=at(z, chip * 2 + 1 - core), device_id_type=MESH)
    for way in range(2):
        @pl.when(z < n_wide - 1 if way == 0 else z > 0)
        def _():
            pl.semaphore_signal(barrier, inc=1, device_id=at(z + 1 - 2 * way, n), device_id_type=MESH)

    load_h = pltpu.make_async_copy(h_hbm, h_in, in_sem.at[0])
    load_k = pltpu.make_async_copy(k_hbm, k_in, in_sem.at[1])
    load_p = pltpu.make_async_copy(phi_hbm, phi, in_sem.at[2])
    tables = [
        pltpu.make_async_copy(a, b, in_sem.at[3 + i])
        for i, (a, b) in enumerate((
            (htiles_hbm, htiles), (ktiles_hbm, ktiles), (rows_hbm, rows), (cols_hbm, cols), (owner_hbm, owner)))
    ]
    tables[0].start()
    tables[4].start()
    load_h.start()
    load_k.start()
    for load in tables[1:4]:
        load.start()
    load_p.start()

    def bf(mask):
        return jnp.where(mask, 1.0, 0.0).astype(jnp.bfloat16)

    def spread(values, extent):
        lane_tile = lax.broadcasted_iota(jnp.int32, (1, extent), 1) // tile
        row = jnp.zeros((1, extent), jnp.int32)
        for a in range(tile_cols):
            row = jnp.where(lane_tile == a, values[a], row)
        return row

    def mask_rows(tiles, b, extent):
        return spread([tiles[a, b] for a in range(tile_cols)], extent).astype(jnp.float32).astype(jnp.bfloat16)

    def tile_span(b):
        return pl.ds(b * tile, tile)

    tables[0].wait()
    tables[4].wait()
    holes = []
    for a in range(tile_cols):
        run, count = htiles[a, 0], htiles[a, 0]
        for b in range(1, tile_rows):
            run = run * htiles[a, b]
            count = count + run
        holes.append(count)
    column = [sum(a * (owner[0, a] == d).astype(jnp.int32) for a in range(tile_cols)) for d in range(n_wide)]
    gaps = [sum(holes[a] * (owner[0, a] == d).astype(jnp.int32) for a in range(tile_cols)) for d in range(n_wide)]
    hole = spread(holes, breadth)
    hole_odd = bf(hole % 2 == 1)
    hole_even = bf(hole % 2 == 0)
    lane_half = lax.broadcasted_iota(jnp.int32, (1, breadth), 1) % tile // short
    halves = [bf(lane_half == 0), bf(lane_half == 1)]
    load_h.wait()
    last = []
    for b in (tile_rows - 2, tile_rows - 1):
        h_in[tile_span(b), :] = h_in[tile_span(b), :] * mask_rows(htiles, b, breadth)
        last.append(h_in[tile_span(b), :])
    left_over = last[0] * hole_odd + last[1] * hole_even
    h_fit[tile_span(tile_rows - 2), :] = left_over * halves[0]
    h_fit[tile_span(tile_rows - 1), :] = left_over * halves[1]
    for b in range(tile_rows - 2):
        value = h_in[tile_span(b), :] * mask_rows(htiles, b, breadth)
        h_in[tile_span(b), :] = value
        h_fit[tile_span(b), :] = value + last[b % 2] * bf(hole == b)

    def pick(each):
        r = lax.broadcasted_iota(jnp.int32, (n_wide * each, breadth), 0)
        col = lax.broadcasted_iota(jnp.int32, (n_wide * each, breadth), 1)
        want = r % each
        for d in range(n_wide):
            want = want + jnp.where(r // each == d, column[d] * tile, 0)
        return want, col

    def turn(which, x):
        return lax.dot_general(which, x, NT, preferred_element_type=jnp.float32).astype(jnp.bfloat16)

    want, col = pick(tile)
    choose = bf(col == want)
    out = turn(choose, h_fit[:tile * (tile_rows - 2), :])
    for d in range(n_wide):
        for q in range(blocks_full):
            start = NOTE + d * unit_rows + q * tile
            pack[z, start:start + tile, :] = out[d * tile:(d + 1) * tile, q * lanes:(q + 1) * lanes]
    want, col = pick(short)
    out = turn(bf((col == want) | (col == want + short)), h_fit[tile * (tile_rows - 2):, :])
    for d in range(n_wide):
        start = NOTE + d * unit_rows + blocks_full * tile
        pack[z, start:start + short, :] = out[d * short:(d + 1) * short]
    note_row = lax.broadcasted_iota(jnp.int32, (NOTE, lanes), 0)
    note = jnp.zeros((NOTE, lanes), jnp.int32)
    for d in range(n_wide):
        note = jnp.where(note_row == d, gaps[d], note)
    note = note.astype(jnp.float32).astype(jnp.bfloat16)
    pack[z, :NOTE, :] = note
    pack[z, end_note:, :] = note

    side = lax.broadcasted_iota(jnp.int32, (1, lanes), 1) // tile
    sidef = side.astype(jnp.float32)

    def lane_block(w, q):
        return pl.ds(pl.multiple_of(w * hrows + q * lanes, lanes), lanes)

    def unfold(g, w):
        above = (w > z).astype(jnp.int32)
        notes = pack[w, pl.ds(pl.multiple_of(above * end_note, NOTE), NOTE), :].astype(jnp.float32)
        for k in range(2):
            gap = jnp.sum(jnp.where(note_row == 2 * g + k, notes, 0.0), axis=0, keepdims=True)
            gap_odd = sum(bf(gap == 2 * i + 1) for i in range(tile_rows // 2))
            gap_even = sum(bf(gap == 2 * i) for i in range(tile_rows // 2))
            start = NOTE + (2 * g + k) * unit_rows
            lone = pack[w, pl.ds(pl.multiple_of(start + blocks_full * tile, NOTE), short), :]
            swapped = pltpu.roll(lone.astype(jnp.float32), tile, 1).astype(jnp.bfloat16)
            moved = None
            top = k * tile
            for q in range(blocks_full):
                x = pack[w, pl.ds(pl.multiple_of(start + q * tile, NOTE), tile), :]
                hit = gap == sidef + 2 * q
                full[g, top:top + tile, lane_block(w, q)] = x * bf(~hit)
                part = x * bf(hit)
                moved = part if moved is None else moved + part
            left = gap_odd * bf(side == 0)
            right = gap_even * bf(side == 1)
            half = top + short
            full[g, top:half, lane_block(w, blocks_full)] = moved[:short] + lone * left + swapped * right
            full[g, half:top + tile, lane_block(w, blocks_full)] = moved[short:] + swapped * left + lone * right

    beside = (z > 0).astype(jnp.int32) + (z < n_wide - 1).astype(jnp.int32)
    pl.semaphore_wait(barrier, len(direct) + 1 + beside)

    def h_copy(u, way, s, src):
        if u == 0:
            start, count = 0 if way == 0 else NOTE + (n_wide - 2) * unit_rows, NOTE + 2 * unit_rows
        else:
            start, count = NOTE + (u + 1 if way == 0 else n_wide - 2 - u) * unit_rows, unit_rows
        ref = pack.at[src, pl.ds(start, count)]
        return pltpu.make_async_remote_copy(
            src_ref=ref, dst_ref=ref, send_sem=h_send.at[u, way, s], recv_sem=h_recv.at[u, way, s],
            device_id=at(z + 1 if way == 0 else z - 1, n), device_id_type=MESH)

    def source(way, s):
        return z - s if way == 0 else z + s

    def has_next(way):
        return z < n_wide - 1 if way == 0 else z > 0

    def has_source(way, s):
        return z >= s if way == 0 else z < n_wide - s

    def h_own(u):
        for way in range(2):
            @pl.when(has_next(way))
            def _():
                h_copy(u, way, 0, z).start()

    def h_pass(u, s):
        for way in range(2):
            @pl.when(has_source(way, s) & has_next(way))
            def _():
                h_copy(u, way, s - 1, source(way, s)).wait_recv()
                h_copy(u, way, s, source(way, s)).start()

    def h_keep(u, s):
        for way in range(2):
            @pl.when(has_source(way, s) & (z == (n_wide - 1 if way == 0 else 0)))
            def _():
                h_copy(u, way, s - 1, source(way, s)).wait_recv()

    def slot(g, c, h):
        return kbuf.at[pl.ds(pl.multiple_of((xor(chip, g, chips) * 2 + c) * kcols + h * hh, hh), hh)]

    def k_copy(g, h, held, to):
        ref = slot(held, core, h)
        return pltpu.make_async_remote_copy(
            src_ref=ref, dst_ref=ref, send_sem=k_send.at[g, h], recv_sem=k_recv.at[g, h],
            device_id=chip_at(to), device_id_type=MESH)

    def k_sent(g, h):
        return k_copy(g, h, 1 + h, 2 - h) if tree and g == 3 else k_copy(g, h, 0, g)

    def sib_copy(g, h, c):
        ref = slot(g, c, h)
        return pltpu.make_async_remote_copy(
            src_ref=ref, dst_ref=ref, send_sem=s_send.at[g, h], recv_sem=s_recv.at[g, h],
            device_id=at(z, chip * 2 + 1 - core), device_id_type=MESH)

    def k_arrive(g, h):
        k_copy(g, h, g, 1).wait_recv()
        if tree and g == 1 + h:
            k_sent(3, h).start()
        sib_copy(g, h, core).start()

    for u in range(n_wide - 1):
        h_own(u)
    tables[1].wait()
    load_k.wait()
    for b in range(tile_rows):
        k_in[tile_span(b), :] = k_in[tile_span(b), :] * mask_rows(ktiles, b, kcols)
    unit = lax.broadcasted_iota(jnp.int32, (kcols, kcols), 0) == lax.broadcasted_iota(jnp.int32, (kcols, kcols), 1)
    kbuf[pl.ds(pl.multiple_of(n * kcols, kcols), kcols), :] = turn(bf(unit), k_in[...])
    order = ((1, 0), (2, 1), (1, 1), (2, 0)) if tree else tuple((g, h) for g in direct for h in range(2))
    for g, h in order:
        k_sent(g, h).start()
    for h in range(2):
        sib_copy(0, h, core).start()
    out = turn(choose, h_in[...])
    for g in range(groups):
        full[g, :, pl.ds(pl.multiple_of(z * hrows, hrows), hrows)] = out[2 * g * tile:2 * (g + 1) * tile]

    kernel_steps = [order[:2], order[2:]] + ([((3, 0), (3, 1))] if tree else [])
    for s in range(1, n_wide - 1):
        for u in range(n_wide - 1):
            h_pass(u, s)
            if kernel_steps and (u, s) in ((0, 1), (1, 1), (0, 2)):
                for g, h in kernel_steps.pop(0):
                    k_arrive(g, h)
    for steps in kernel_steps:
        for g, h in steps:
            k_arrive(g, h)

    first_near = z // (n_wide - 1)
    far = (n_wide - 1) * (1 - first_near)

    upper = z // (n_wide // 2)
    lane = lax.broadcasted_iota(jnp.int32, (1, lanes), 1)
    low = lane < tile

    def group(i):
        return upper * i + (1 - upper) * (groups - 1 - i)

    def product(g, w, count):
        span = pl.ds(pl.multiple_of(w * hrows, hrows), count * hrows)
        return jnp.dot(full[g, :, span], kbuf[span, :], preferred_element_type=jnp.float32)

    def keeps(i):
        return (0,) if i == 0 else (2 * i - 1, 2 * i)

    def ready(i):
        for u in keeps(i):
            for s in range(1, n_wide - 1):
                h_keep(u, s)

        def step(w, carry):
            @pl.when(w != z)
            def _():
                unfold(group(i), w)

            return carry

        lax.fori_loop(first_near, first_near + n_wide - 1, step, 0)

    def slot_of(src, dst):
        return (src - dst + n_wide) % n_wide - 1

    own_copy = pltpu.make_async_copy(own, own_out, own_sem)

    def r_copy(i, k):
        there = slot_of(z, 2 * group(i) + k)
        return pltpu.make_async_remote_copy(
            src_ref=stage.at[2 * i + k], dst_ref=landed.at[there], send_sem=r_send.at[2 * i + k], recv_sem=r_recv.at[there],
            device_id=at(2 * group(i) + k, n), device_id_type=MESH)

    def r_wait(s):
        pltpu.make_async_remote_copy(
            src_ref=stage.at[0], dst_ref=landed.at[s - 1], send_sem=r_send.at[0], recv_sem=r_recv.at[s - 1],
            device_id=at((z + s) % n_wide, n), device_id_type=MESH).wait_recv()

    def finish(i):
        g = group(i)
        for b2 in range(tile_rows // 2):
            x = acc[:, lanes * b2:lanes * (b2 + 1)]
            y = pltpu.roll(x, tile, 1)
            table[2 * b2] = jnp.where(low, x, y).astype(jnp.bfloat16)
            table[2 * b2 + 1] = jnp.where(low, y, x).astype(jnp.bfloat16)

        def place(t, carry):
            to = [owner[0, cols[2 * t + side]] for side in range(2)]
            at_lane = pl.ds(pl.multiple_of(t * lanes, lanes), lanes)
            for k in range(2):
                kept = [(one == 2 * g + k).astype(jnp.int32) for one in to]
                left = jnp.where(low, kept[0], 0).astype(jnp.float32).astype(jnp.bfloat16)
                right = jnp.where(low, 0, kept[1]).astype(jnp.float32).astype(jnp.bfloat16)
                span = pl.ds(k * tile, tile)
                lhs[span, at_lane] = table[rows[2 * t], span] * left + table[rows[2 * t + 1], span] * right
            return carry

        lax.fori_loop(0, pairs // 2, place, 0, unroll=4)
        return jnp.dot(lhs[...], phi[...], preferred_element_type=jnp.float32)

    def chunk(i):
        if i > 0:
            ready(i)
        g = group(i)
        acc[...] = product(g, first_near, n_wide - 1)
        for u in keeps(i):
            h_keep(u, n_wide - 1)
        unfold(g, far)
        acc[...] += product(g, far, 1)
        blocks = finish(i)
        for k in range(2):
            block = blocks[k * tile:(k + 1) * tile]

            @pl.when(2 * g + k == z)
            def _():
                own[...] = block
                own_copy.start()

            @pl.when(2 * g + k != z)
            def _():
                stage[2 * i + k] = block.astype(jnp.bfloat16)
                r_copy(i, k).start()

    ready(0)
    for g in range(chips):
        for h in range(2):
            sib_copy(g, h, 1 - core).wait_recv()
    load_p.wait()
    for load in tables[2:4]:
        load.wait()
    for i in range(groups):
        chunk(i)

    own_copy.wait()
    for s in range(1, n_wide):
        r_wait(s)

    for i in range(groups):
        for k in range(2):
            @pl.when(2 * group(i) + k != z)
            def _():
                r_copy(i, k).wait_send()
    for g in range(1, chips):
        for h in range(2):
            k_sent(g, h).wait_send()
    for g in range(chips):
        for h in range(2):
            sib_copy(g, h, core).wait_send()
    for u in range(n_wide - 1):
        for way in range(2):
            for s in range(n_wide - 1):
                @pl.when(has_next(way) & has_source(way, s))
                def _():
                    h_copy(u, way, s, source(way, s)).wait_send()


def body(n_wide, n_narrow, kernel, hamiltonian, kernel_tiles, ham_tiles, pair_row, pair_col, sphere_phi, owner):
    pairs, tile, pts = sphere_phi.shape
    height, kcols = kernel.shape
    hrows, breadth = hamiltonian.shape
    tile_rows, tile_cols = ham_tiles.shape
    chips = n_narrow // 2
    hbm = pl.BlockSpec(memory_space=pltpu.HBM)
    dma = pltpu.SemaphoreType.DMA
    unit_rows = (tile_rows // 2 - 1) * tile + tile // 2
    bf16 = jnp.bfloat16

    own, landed = pl.pallas_call(
        functools.partial(kernel_body, n_wide, n_narrow, tile),
        out_shape=(
            jax.ShapeDtypeStruct((tile, pts), jnp.float32),
            jax.ShapeDtypeStruct((n_wide - 1, tile, pts), bf16)),
        in_specs=[hbm] * 8,
        out_specs=(hbm, hbm),
        scratch_shapes=[
            pltpu.SMEM((tile_cols, tile_rows), jnp.int32),
            pltpu.SMEM((tile_cols, tile_rows), jnp.int32),
            pltpu.SMEM((pairs,), jnp.int32),
            pltpu.SMEM((pairs,), jnp.int32),
            pltpu.SMEM((1, tile_cols), jnp.int32),
            pltpu.VMEM((height, kcols), bf16),
            pltpu.VMEM((hrows, breadth), bf16),
            pltpu.VMEM((hrows, breadth), bf16),
            pltpu.VMEM((pairs * tile, pts), bf16),
            pltpu.VMEM((n_narrow * kcols, height), bf16),
            pltpu.VMEM((n_wide // 2, 2 * tile, n_wide * hrows), bf16),
            pltpu.VMEM((n_wide, n_wide * unit_rows + 2 * NOTE, 2 * tile), bf16),
            pltpu.VMEM((2 * tile, height), jnp.float32),
            pltpu.VMEM((tile_rows, 2 * tile, 2 * tile), bf16),
            pltpu.VMEM((2 * tile, pairs * tile), bf16),
            pltpu.VMEM((tile, pts), jnp.float32),
            pltpu.VMEM((n_wide, tile, pts), bf16),
            dma((8,)), dma(()),
            dma((chips, 2)), dma((chips, 2)),
            dma((chips, 2)), dma((chips, 2)),
            dma((n_wide, 2, n_wide)), dma((n_wide, 2, n_wide)),
            dma((n_wide,)), dma((n_wide,)),
        ],
        compiler_params=pltpu.CompilerParams(
            collective_id=0, has_side_effects=True, vmem_limit_bytes=60 * 2**20),
    )(kernel_tiles.T, ham_tiles.T, pair_row, pair_col, owner, kernel, hamiltonian,
      sphere_phi.reshape(pairs * tile, pts))
    for s in range(n_wide - 1):
        own = own + landed[s].astype(jnp.float32)
    return own[None]


def solution(mesh):
    return jax.shard_map(
        functools.partial(body, mesh.shape["wide"], mesh.shape["narrow"]),
        mesh=mesh,
        in_specs=(
            P("wide", "narrow"),
            P("wide", "narrow"),
            P("wide", "narrow"),
            P("wide", "narrow"),
            P(("wide", "narrow")),
            P(("wide", "narrow")),
            P(("wide", "narrow"), None, None),
            P("narrow", None),
        ),
        out_specs=P(("wide", "narrow"), None, None),
        check_vma=False,
    )
```

```python
import functools

import jax
import jax.numpy as jnp
from jax import lax
from jax.experimental import pallas as pl
from jax.experimental.pallas import tpu as pltpu
from jax.sharding import PartitionSpec as P

MESH = pl.DeviceIdType.MESH
NT = (((1,), (1,)), ((), ()))


NOTE = 16


def xor(a, b, size):
    total, bit = 0, 1
    while bit < size:
        total = total + ((a // bit + b // bit) % 2) * bit
        bit *= 2
    return total


def kernel_body(
    n_wide, n_narrow, tile,
    ktiles_hbm, htiles_hbm, rows_hbm, cols_hbm, owner_hbm, k_hbm, h_hbm, phi_hbm, own_out, landed,
    ktiles, htiles, rows, cols, owner, k_in, h_in, h_fit, phi, kbuf, full, pack,
    acc, table, lhs, own, stage,
    in_sem, own_sem, k_send, k_recv, s_send, s_recv, h_send, h_recv, r_send, r_recv,
):
    z = lax.axis_index("wide")
    n = lax.axis_index("narrow")
    chips = n_narrow // 2
    chip, core = n // 2, n % 2
    tile_cols, tile_rows = htiles.shape
    height, kcols = k_hbm.shape
    hrows, breadth = h_hbm.shape
    per = hrows // kcols
    pairs = rows.shape[0]
    lanes = 2 * tile
    blocks_full = tile_rows // 2 - 1
    short = tile // 2
    unit_rows = blocks_full * tile + short
    end_note = NOTE + n_wide * unit_rows
    groups = n_wide // 2
    tree = chips == 4
    hh = kcols // 2

    barrier = pltpu.get_barrier_semaphore()

    def at(w, m):
        return (w, m)

    def chip_at(g):
        return at(z, xor(chip, g, chips) * 2 + core)

    direct = (1, 2) if tree else tuple(range(1, chips))
    for g in direct:
        pl.semaphore_signal(barrier, inc=1, device_id=chip_at(g), device_id_type=MESH)
    pl.semaphore_signal(barrier, inc=1, device_id=at(z, chip * 2 + 1 - core), device_id_type=MESH)
    for way in range(2):
        @pl.when(z < n_wide - 1 if way == 0 else z > 0)
        def _():
            pl.semaphore_signal(barrier, inc=1, device_id=at(z + 1 - 2 * way, n), device_id_type=MESH)

    load_h = pltpu.make_async_copy(h_hbm, h_in, in_sem.at[0])
    load_k = pltpu.make_async_copy(k_hbm, k_in, in_sem.at[1])
    load_p = pltpu.make_async_copy(phi_hbm, phi, in_sem.at[2])
    tables = [
        pltpu.make_async_copy(a, b, in_sem.at[3 + i])
        for i, (a, b) in enumerate((
            (htiles_hbm, htiles), (ktiles_hbm, ktiles), (rows_hbm, rows), (cols_hbm, cols), (owner_hbm, owner)))
    ]
    tables[0].start()
    tables[4].start()
    load_h.start()
    load_k.start()
    for load in tables[1:4]:
        load.start()
    load_p.start()

    def bf(mask):
        return jnp.where(mask, 1.0, 0.0).astype(jnp.bfloat16)

    def spread(values, extent):
        lane_tile = lax.broadcasted_iota(jnp.int32, (1, extent), 1) // tile
        row = jnp.zeros((1, extent), jnp.int32)
        for a in range(tile_cols):
            row = jnp.where(lane_tile == a, values[a], row)
        return row

    def mask_rows(tiles, b, extent):
        return spread([tiles[a, b] for a in range(tile_cols)], extent).astype(jnp.float32).astype(jnp.bfloat16)

    def tile_span(b):
        return pl.ds(b * tile, tile)

    tables[0].wait()
    tables[4].wait()
    holes = []
    for a in range(tile_cols):
        run, count = htiles[a, 0], htiles[a, 0]
        for b in range(1, tile_rows):
            run = run * htiles[a, b]
            count = count + run
        holes.append(count)
    column = [sum(a * (owner[0, a] == d).astype(jnp.int32) for a in range(tile_cols)) for d in range(n_wide)]
    gaps = [sum(holes[a] * (owner[0, a] == d).astype(jnp.int32) for a in range(tile_cols)) for d in range(n_wide)]
    hole = spread(holes, breadth)
    hole_odd = bf(hole % 2 == 1)
    hole_even = bf(hole % 2 == 0)
    lane_half = lax.broadcasted_iota(jnp.int32, (1, breadth), 1) % tile // short
    halves = [bf(lane_half == 0), bf(lane_half == 1)]
    load_h.wait()
    last = []
    for b in (tile_rows - 2, tile_rows - 1):
        h_in[tile_span(b), :] = h_in[tile_span(b), :] * mask_rows(htiles, b, breadth)
        last.append(h_in[tile_span(b), :])
    left_over = last[0] * hole_odd + last[1] * hole_even
    h_fit[tile_span(tile_rows - 2), :] = left_over * halves[0]
    h_fit[tile_span(tile_rows - 1), :] = left_over * halves[1]
    for b in range(tile_rows - 2):
        value = h_in[tile_span(b), :] * mask_rows(htiles, b, breadth)
        h_in[tile_span(b), :] = value
        h_fit[tile_span(b), :] = value + last[b % 2] * bf(hole == b)

    def pick(each):
        r = lax.broadcasted_iota(jnp.int32, (n_wide * each, breadth), 0)
        col = lax.broadcasted_iota(jnp.int32, (n_wide * each, breadth), 1)
        want = r % each
        for d in range(n_wide):
            want = want + jnp.where(r // each == d, column[d] * tile, 0)
        return want, col

    def turn(which, x):
        return lax.dot_general(which, x, NT, preferred_element_type=jnp.float32).astype(jnp.bfloat16)

    want, col = pick(tile)
    choose = bf(col == want)
    out = turn(choose, h_fit[:tile * (tile_rows - 2), :])
    for d in range(n_wide):
        for q in range(blocks_full):
            start = NOTE + d * unit_rows + q * tile
            pack[z, start:start + tile, :] = out[d * tile:(d + 1) * tile, q * lanes:(q + 1) * lanes]
    want, col = pick(short)
    out = turn(bf((col == want) | (col == want + short)), h_fit[tile * (tile_rows - 2):, :])
    for d in range(n_wide):
        start = NOTE + d * unit_rows + blocks_full * tile
        pack[z, start:start + short, :] = out[d * short:(d + 1) * short]
    note_row = lax.broadcasted_iota(jnp.int32, (NOTE, lanes), 0)
    note = jnp.zeros((NOTE, lanes), jnp.int32)
    for d in range(n_wide):
        note = jnp.where(note_row == d, gaps[d], note)
    note = note.astype(jnp.float32).astype(jnp.bfloat16)
    pack[z, :NOTE, :] = note
    pack[z, end_note:, :] = note

    side = lax.broadcasted_iota(jnp.int32, (1, lanes), 1) // tile
    sidef = side.astype(jnp.float32)

    def lane_block(w, q):
        return pl.ds(pl.multiple_of(w * hrows + q * lanes, lanes), lanes)

    def unfold(g, w):
        above = (w > z).astype(jnp.int32)
        notes = pack[w, pl.ds(pl.multiple_of(above * end_note, NOTE), NOTE), :].astype(jnp.float32)
        for k in range(2):
            gap = jnp.sum(jnp.where(note_row == 2 * g + k, notes, 0.0), axis=0, keepdims=True)
            gap_odd = sum(bf(gap == 2 * i + 1) for i in range(tile_rows // 2))
            gap_even = sum(bf(gap == 2 * i) for i in range(tile_rows // 2))
            start = NOTE + (2 * g + k) * unit_rows
            lone = pack[w, pl.ds(pl.multiple_of(start + blocks_full * tile, NOTE), short), :]
            swapped = pltpu.roll(lone.astype(jnp.float32), tile, 1).astype(jnp.bfloat16)
            moved = None
            top = k * tile
            for q in range(blocks_full):
                x = pack[w, pl.ds(pl.multiple_of(start + q * tile, NOTE), tile), :]
                hit = gap == sidef + 2 * q
                full[g, top:top + tile, lane_block(w, q)] = x * bf(~hit)
                part = x * bf(hit)
                moved = part if moved is None else moved + part
            left = gap_odd * bf(side == 0)
            right = gap_even * bf(side == 1)
            half = top + short
            full[g, top:half, lane_block(w, blocks_full)] = moved[:short] + lone * left + swapped * right
            full[g, half:top + tile, lane_block(w, blocks_full)] = moved[short:] + swapped * left + lone * right

    beside = (z > 0).astype(jnp.int32) + (z < n_wide - 1).astype(jnp.int32)
    pl.semaphore_wait(barrier, len(direct) + 1 + beside)

    def h_copy(u, way, s, src):
        if u == 0:
            start, count = 0 if way == 0 else NOTE + (n_wide - 2) * unit_rows, NOTE + 2 * unit_rows
        else:
            start, count = NOTE + (u + 1 if way == 0 else n_wide - 2 - u) * unit_rows, unit_rows
        ref = pack.at[src, pl.ds(start, count)]
        return pltpu.make_async_remote_copy(
            src_ref=ref, dst_ref=ref, send_sem=h_send.at[u, way, s], recv_sem=h_recv.at[u, way, s],
            device_id=at(z + 1 if way == 0 else z - 1, n), device_id_type=MESH)

    def source(way, s):
        return z - s if way == 0 else z + s

    def has_next(way):
        return z < n_wide - 1 if way == 0 else z > 0

    def has_source(way, s):
        return z >= s if way == 0 else z < n_wide - s

    def h_own(u):
        for way in range(2):
            @pl.when(has_next(way))
            def _():
                h_copy(u, way, 0, z).start()

    def h_pass(u, s):
        for way in range(2):
            @pl.when(has_source(way, s) & has_next(way))
            def _():
                h_copy(u, way, s - 1, source(way, s)).wait_recv()
                h_copy(u, way, s, source(way, s)).start()

    def h_keep(u, s):
        for way in range(2):
            @pl.when(has_source(way, s) & (z == (n_wide - 1 if way == 0 else 0)))
            def _():
                h_copy(u, way, s - 1, source(way, s)).wait_recv()

    def slot(g, c, h):
        return kbuf.at[pl.ds(pl.multiple_of((xor(chip, g, chips) * 2 + c) * kcols + h * hh, hh), hh)]

    def k_copy(g, h, held, to):
        ref = slot(held, core, h)
        return pltpu.make_async_remote_copy(
            src_ref=ref, dst_ref=ref, send_sem=k_send.at[g, h], recv_sem=k_recv.at[g, h],
            device_id=chip_at(to), device_id_type=MESH)

    def k_sent(g, h):
        return k_copy(g, h, 1 + h, 2 - h) if tree and g == 3 else k_copy(g, h, 0, g)

    def sib_copy(g, h, c):
        ref = slot(g, c, h)
        return pltpu.make_async_remote_copy(
            src_ref=ref, dst_ref=ref, send_sem=s_send.at[g, h], recv_sem=s_recv.at[g, h],
            device_id=at(z, chip * 2 + 1 - core), device_id_type=MESH)

    def k_arrive(g, h):
        k_copy(g, h, g, 1).wait_recv()
        if tree and g == 1 + h:
            k_sent(3, h).start()
        sib_copy(g, h, core).start()

    for u in range(n_wide - 1):
        h_own(u)
    tables[1].wait()
    load_k.wait()
    for b in range(tile_rows):
        k_in[tile_span(b), :] = k_in[tile_span(b), :] * mask_rows(ktiles, b, kcols)
    unit = lax.broadcasted_iota(jnp.int32, (kcols, kcols), 0) == lax.broadcasted_iota(jnp.int32, (kcols, kcols), 1)
    kbuf[pl.ds(pl.multiple_of(n * kcols, kcols), kcols), :] = turn(bf(unit), k_in[...])
    order = ((1, 0), (2, 1), (1, 1), (2, 0)) if tree else tuple((g, h) for g in direct for h in range(2))
    for g, h in order:
        k_sent(g, h).start()
    for h in range(2):
        sib_copy(0, h, core).start()
    out = turn(choose, h_in[...])
    for g in range(groups):
        full[g, :, pl.ds(pl.multiple_of(z * hrows, hrows), hrows)] = out[2 * g * tile:2 * (g + 1) * tile]

    kernel_steps = [order[:2], order[2:]] + ([((3, 0), (3, 1))] if tree else [])
    for s in range(1, n_wide - 1):
        for u in range(n_wide - 1):
            h_pass(u, s)
            if kernel_steps and (u, s) in ((0, 1), (1, 1), (0, 2)):
                for g, h in kernel_steps.pop(0):
                    k_arrive(g, h)
    for steps in kernel_steps:
        for g, h in steps:
            k_arrive(g, h)

    first_near = z // (n_wide - 1)
    far = (n_wide - 1) * (1 - first_near)

    upper = z // (n_wide // 2)
    lane = lax.broadcasted_iota(jnp.int32, (1, lanes), 1)
    low = lane < tile

    def group(i):
        return upper * i + (1 - upper) * (groups - 1 - i)

    def product(g, w, count):
        span = pl.ds(pl.multiple_of(w * hrows, hrows), count * hrows)
        return jnp.dot(full[g, :, span], kbuf[span, :], preferred_element_type=jnp.float32)

    def keeps(i):
        return (0,) if i == 0 else (2 * i - 1, 2 * i)

    def ready(i):
        for u in keeps(i):
            for s in range(1, n_wide - 1):
                h_keep(u, s)

        def step(w, carry):
            @pl.when(w != z)
            def _():
                unfold(group(i), w)

            return carry

        lax.fori_loop(first_near, first_near + n_wide - 1, step, 0)

    def slot_of(src, dst):
        return (src - dst + n_wide) % n_wide - 1

    own_copy = pltpu.make_async_copy(own, own_out, own_sem)

    def r_copy(i, k):
        there = slot_of(z, 2 * group(i) + k)
        return pltpu.make_async_remote_copy(
            src_ref=stage.at[2 * i + k], dst_ref=landed.at[there], send_sem=r_send.at[2 * i + k], recv_sem=r_recv.at[there],
            device_id=at(2 * group(i) + k, n), device_id_type=MESH)

    def r_wait(s):
        pltpu.make_async_remote_copy(
            src_ref=stage.at[0], dst_ref=landed.at[s - 1], send_sem=r_send.at[0], recv_sem=r_recv.at[s - 1],
            device_id=at((z + s) % n_wide, n), device_id_type=MESH).wait_recv()

    def finish(i):
        g = group(i)
        for b2 in range(tile_rows // 2):
            x = acc[:, lanes * b2:lanes * (b2 + 1)]
            y = pltpu.roll(x, tile, 1)
            table[2 * b2] = jnp.where(low, x, y).astype(jnp.bfloat16)
            table[2 * b2 + 1] = jnp.where(low, y, x).astype(jnp.bfloat16)

        def place(t):
            to = [owner[0, cols[2 * t + side]] for side in range(2)]
            at_lane = pl.ds(t * lanes, lanes)
            for k in range(2):
                kept = [(one == 2 * g + k).astype(jnp.int32) for one in to]
                left = jnp.where(low, kept[0], 0).astype(jnp.float32).astype(jnp.bfloat16)
                right = jnp.where(low, 0, kept[1]).astype(jnp.float32).astype(jnp.bfloat16)
                span = pl.ds(k * tile, tile)
                lhs[span, at_lane] = table[rows[2 * t], span] * left + table[rows[2 * t + 1], span] * right

        for t in range(pairs // 2):
            place(t)
        return jnp.dot(lhs[...], phi[...], preferred_element_type=jnp.float32)

    def chunk(i):
        if i > 0:
            ready(i)
        g = group(i)
        acc[...] = product(g, first_near, n_wide - 1)
        for u in keeps(i):
            h_keep(u, n_wide - 1)
        unfold(g, far)
        acc[...] += product(g, far, 1)
        blocks = finish(i)
        for k in range(2):
            block = blocks[k * tile:(k + 1) * tile]

            @pl.when(2 * g + k == z)
            def _():
                own[...] = block
                own_copy.start()

            @pl.when(2 * g + k != z)
            def _():
                stage[2 * i + k] = block.astype(jnp.bfloat16)
                r_copy(i, k).start()

    ready(0)
    for g in range(chips):
        for h in range(2):
            sib_copy(g, h, 1 - core).wait_recv()
    load_p.wait()
    for load in tables[2:4]:
        load.wait()
    for i in range(groups):
        chunk(i)

    own_copy.wait()
    for s in range(1, n_wide):
        r_wait(s)

    for i in range(groups):
        for k in range(2):
            @pl.when(2 * group(i) + k != z)
            def _():
                r_copy(i, k).wait_send()
    for g in range(1, chips):
        for h in range(2):
            k_sent(g, h).wait_send()
    for g in range(chips):
        for h in range(2):
            sib_copy(g, h, core).wait_send()
    for u in range(n_wide - 1):
        for way in range(2):
            for s in range(n_wide - 1):
                @pl.when(has_next(way) & has_source(way, s))
                def _():
                    h_copy(u, way, s, source(way, s)).wait_send()


def body(n_wide, n_narrow, kernel, hamiltonian, kernel_tiles, ham_tiles, pair_row, pair_col, sphere_phi, owner):
    pairs, tile, pts = sphere_phi.shape
    height, kcols = kernel.shape
    hrows, breadth = hamiltonian.shape
    tile_rows, tile_cols = ham_tiles.shape
    chips = n_narrow // 2
    hbm = pl.BlockSpec(memory_space=pltpu.HBM)
    dma = pltpu.SemaphoreType.DMA
    unit_rows = (tile_rows // 2 - 1) * tile + tile // 2
    bf16 = jnp.bfloat16

    own, landed = pl.pallas_call(
        functools.partial(kernel_body, n_wide, n_narrow, tile),
        out_shape=(
            jax.ShapeDtypeStruct((tile, pts), jnp.float32),
            jax.ShapeDtypeStruct((n_wide - 1, tile, pts), bf16)),
        in_specs=[hbm] * 8,
        out_specs=(hbm, hbm),
        scratch_shapes=[
            pltpu.SMEM((tile_cols, tile_rows), jnp.int32),
            pltpu.SMEM((tile_cols, tile_rows), jnp.int32),
            pltpu.SMEM((pairs,), jnp.int32),
            pltpu.SMEM((pairs,), jnp.int32),
            pltpu.SMEM((1, tile_cols), jnp.int32),
            pltpu.VMEM((height, kcols), bf16),
            pltpu.VMEM((hrows, breadth), bf16),
            pltpu.VMEM((hrows, breadth), bf16),
            pltpu.VMEM((pairs * tile, pts), bf16),
            pltpu.VMEM((n_narrow * kcols, height), bf16),
            pltpu.VMEM((n_wide // 2, 2 * tile, n_wide * hrows), bf16),
            pltpu.VMEM((n_wide, n_wide * unit_rows + 2 * NOTE, 2 * tile), bf16),
            pltpu.VMEM((2 * tile, height), jnp.float32),
            pltpu.VMEM((tile_rows, 2 * tile, 2 * tile), bf16),
            pltpu.VMEM((2 * tile, pairs * tile), bf16),
            pltpu.VMEM((tile, pts), jnp.float32),
            pltpu.VMEM((n_wide, tile, pts), bf16),
            dma((8,)), dma(()),
            dma((chips, 2)), dma((chips, 2)),
            dma((chips, 2)), dma((chips, 2)),
            dma((n_wide, 2, n_wide)), dma((n_wide, 2, n_wide)),
            dma((n_wide,)), dma((n_wide,)),
        ],
        compiler_params=pltpu.CompilerParams(
            collective_id=0, has_side_effects=True, vmem_limit_bytes=60 * 2**20),
    )(kernel_tiles.T, ham_tiles.T, pair_row, pair_col, owner, kernel, hamiltonian,
      sphere_phi.reshape(pairs * tile, pts))
    for s in range(n_wide - 1):
        own = own + landed[s].astype(jnp.float32)
    return own[None]


def solution(mesh):
    return jax.shard_map(
        functools.partial(body, mesh.shape["wide"], mesh.shape["narrow"]),
        mesh=mesh,
        in_specs=(
            P("wide", "narrow"),
            P("wide", "narrow"),
            P("wide", "narrow"),
            P("wide", "narrow"),
            P(("wide", "narrow")),
            P(("wide", "narrow")),
            P(("wide", "narrow"), None, None),
            P("narrow", None),
        ),
        out_specs=P(("wide", "narrow"), None, None),
        check_vma=False,
    )
```

```python
import functools

import jax
import jax.numpy as jnp
from jax import lax
from jax.experimental import pallas as pl
from jax.experimental.pallas import tpu as pltpu
from jax.sharding import PartitionSpec as P

MESH = pl.DeviceIdType.MESH
NT = (((1,), (1,)), ((), ()))


NOTE = 16


def xor(a, b, size):
    total, bit = 0, 1
    while bit < size:
        total = total + ((a // bit + b // bit) % 2) * bit
        bit *= 2
    return total


def kernel_body(
    n_wide, n_narrow, tile,
    ktiles_hbm, htiles_hbm, rows_hbm, cols_hbm, owner_hbm, k_hbm, h_hbm, phi_hbm, own_out, landed,
    ktiles, htiles, rows, cols, owner, k_in, h_in, h_fit, phi, kbuf, full, pack,
    acc, table, lhs, own, stage,
    in_sem, own_sem, k_send, k_recv, s_send, s_recv, h_send, h_recv, r_send, r_recv,
):
    z = lax.axis_index("wide")
    n = lax.axis_index("narrow")
    chips = n_narrow // 2
    chip, core = n // 2, n % 2
    tile_cols, tile_rows = htiles.shape
    height, kcols = k_hbm.shape
    hrows, breadth = h_hbm.shape
    per = hrows // kcols
    pairs = rows.shape[0]
    lanes = 2 * tile
    blocks_full = tile_rows // 2 - 1
    short = tile // 2
    unit_rows = blocks_full * tile + short
    end_note = NOTE + n_wide * unit_rows
    groups = n_wide // 2
    tree = chips == 4
    hh = kcols // 2

    barrier = pltpu.get_barrier_semaphore()

    def at(w, m):
        return (w, m)

    def chip_at(g):
        return at(z, xor(chip, g, chips) * 2 + core)

    direct = (1, 2) if tree else tuple(range(1, chips))
    for g in direct:
        pl.semaphore_signal(barrier, inc=1, device_id=chip_at(g), device_id_type=MESH)
    pl.semaphore_signal(barrier, inc=1, device_id=at(z, chip * 2 + 1 - core), device_id_type=MESH)
    for way in range(2):
        @pl.when(z < n_wide - 1 if way == 0 else z > 0)
        def _():
            pl.semaphore_signal(barrier, inc=1, device_id=at(z + 1 - 2 * way, n), device_id_type=MESH)

    load_h = pltpu.make_async_copy(h_hbm, h_in, in_sem.at[0])
    load_k = pltpu.make_async_copy(k_hbm, k_in, in_sem.at[1])
    load_p = pltpu.make_async_copy(phi_hbm, phi, in_sem.at[2])
    tables = [
        pltpu.make_async_copy(a, b, in_sem.at[3 + i])
        for i, (a, b) in enumerate((
            (htiles_hbm, htiles), (ktiles_hbm, ktiles), (rows_hbm, rows), (cols_hbm, cols), (owner_hbm, owner)))
    ]
    tables[0].start()
    tables[4].start()
    load_h.start()
    load_k.start()
    for load in tables[1:4]:
        load.start()
    load_p.start()

    def bf(mask):
        return jnp.where(mask, 1.0, 0.0).astype(jnp.bfloat16)

    def spread(values, extent):
        lane_tile = lax.broadcasted_iota(jnp.int32, (1, extent), 1) // tile
        row = jnp.zeros((1, extent), jnp.int32)
        for a in range(tile_cols):
            row = jnp.where(lane_tile == a, values[a], row)
        return row

    def mask_rows(tiles, b, extent):
        return spread([tiles[a, b] for a in range(tile_cols)], extent).astype(jnp.float32).astype(jnp.bfloat16)

    def tile_span(b):
        return pl.ds(b * tile, tile)

    tables[0].wait()
    tables[4].wait()
    holes = []
    for a in range(tile_cols):
        run, count = htiles[a, 0], htiles[a, 0]
        for b in range(1, tile_rows):
            run = run * htiles[a, b]
            count = count + run
        holes.append(count)
    column = [sum(a * (owner[0, a] == d).astype(jnp.int32) for a in range(tile_cols)) for d in range(n_wide)]
    gaps = [sum(holes[a] * (owner[0, a] == d).astype(jnp.int32) for a in range(tile_cols)) for d in range(n_wide)]
    hole = spread(holes, breadth)
    hole_odd = bf(hole % 2 == 1)
    hole_even = bf(hole % 2 == 0)
    lane_half = lax.broadcasted_iota(jnp.int32, (1, breadth), 1) % tile // short
    halves = [bf(lane_half == 0), bf(lane_half == 1)]
    load_h.wait()
    last = []
    for b in (tile_rows - 2, tile_rows - 1):
        h_in[tile_span(b), :] = h_in[tile_span(b), :] * mask_rows(htiles, b, breadth)
        last.append(h_in[tile_span(b), :])
    left_over = last[0] * hole_odd + last[1] * hole_even
    h_fit[tile_span(tile_rows - 2), :] = left_over * halves[0]
    h_fit[tile_span(tile_rows - 1), :] = left_over * halves[1]
    for b in range(tile_rows - 2):
        value = h_in[tile_span(b), :] * mask_rows(htiles, b, breadth)
        h_in[tile_span(b), :] = value
        h_fit[tile_span(b), :] = value + last[b % 2] * bf(hole == b)

    def pick(each):
        r = lax.broadcasted_iota(jnp.int32, (n_wide * each, breadth), 0)
        col = lax.broadcasted_iota(jnp.int32, (n_wide * each, breadth), 1)
        want = r % each
        for d in range(n_wide):
            want = want + jnp.where(r // each == d, column[d] * tile, 0)
        return want, col

    def turn(which, x):
        return lax.dot_general(which, x, NT, preferred_element_type=jnp.float32).astype(jnp.bfloat16)

    want, col = pick(tile)
    choose = bf(col == want)
    out = turn(choose, h_fit[:tile * (tile_rows - 2), :])
    for d in range(n_wide):
        for q in range(blocks_full):
            start = NOTE + d * unit_rows + q * tile
            pack[z, start:start + tile, :] = out[d * tile:(d + 1) * tile, q * lanes:(q + 1) * lanes]
    want, col = pick(short)
    out = turn(bf((col == want) | (col == want + short)), h_fit[tile * (tile_rows - 2):, :])
    for d in range(n_wide):
        start = NOTE + d * unit_rows + blocks_full * tile
        pack[z, start:start + short, :] = out[d * short:(d + 1) * short]
    note_row = lax.broadcasted_iota(jnp.int32, (NOTE, lanes), 0)
    note = jnp.zeros((NOTE, lanes), jnp.int32)
    for d in range(n_wide):
        note = jnp.where(note_row == d, gaps[d], note)
    note = note.astype(jnp.float32).astype(jnp.bfloat16)
    pack[z, :NOTE, :] = note
    pack[z, end_note:, :] = note

    side = lax.broadcasted_iota(jnp.int32, (1, lanes), 1) // tile
    sidef = side.astype(jnp.float32)

    def lane_block(w, q):
        return pl.ds(pl.multiple_of(w * hrows + q * lanes, lanes), lanes)

    def unfold(g, w):
        above = (w > z).astype(jnp.int32)
        notes = pack[w, pl.ds(pl.multiple_of(above * end_note, NOTE), NOTE), :].astype(jnp.float32)
        for k in range(2):
            gap = jnp.sum(jnp.where(note_row == 2 * g + k, notes, 0.0), axis=0, keepdims=True)
            gap_odd = sum(bf(gap == 2 * i + 1) for i in range(tile_rows // 2))
            gap_even = sum(bf(gap == 2 * i) for i in range(tile_rows // 2))
            start = NOTE + (2 * g + k) * unit_rows
            lone = pack[w, pl.ds(pl.multiple_of(start + blocks_full * tile, NOTE), short), :]
            swapped = pltpu.roll(lone.astype(jnp.float32), tile, 1).astype(jnp.bfloat16)
            moved = None
            top = k * tile
            for q in range(blocks_full):
                x = pack[w, pl.ds(pl.multiple_of(start + q * tile, NOTE), tile), :]
                hit = gap == sidef + 2 * q
                full[g, top:top + tile, lane_block(w, q)] = x * bf(~hit)
                part = x * bf(hit)
                moved = part if moved is None else moved + part
            left = gap_odd * bf(side == 0)
            right = gap_even * bf(side == 1)
            half = top + short
            full[g, top:half, lane_block(w, blocks_full)] = moved[:short] + lone * left + swapped * right
            full[g, half:top + tile, lane_block(w, blocks_full)] = moved[short:] + swapped * left + lone * right

    beside = (z > 0).astype(jnp.int32) + (z < n_wide - 1).astype(jnp.int32)
    pl.semaphore_wait(barrier, len(direct) + 1 + beside)

    def h_copy(u, way, s, src):
        if u == 0:
            start, count = 0 if way == 0 else NOTE + (n_wide - 2) * unit_rows, NOTE + 2 * unit_rows
        else:
            start, count = NOTE + (u + 1 if way == 0 else n_wide - 2 - u) * unit_rows, unit_rows
        ref = pack.at[src, pl.ds(start, count)]
        return pltpu.make_async_remote_copy(
            src_ref=ref, dst_ref=ref, send_sem=h_send.at[u, way, s], recv_sem=h_recv.at[u, way, s],
            device_id=at(z + 1 if way == 0 else z - 1, n), device_id_type=MESH)

    def source(way, s):
        return z - s if way == 0 else z + s

    def has_next(way):
        return z < n_wide - 1 if way == 0 else z > 0

    def has_source(way, s):
        return z >= s if way == 0 else z < n_wide - s

    def h_own(u):
        for way in range(2):
            @pl.when(has_next(way))
            def _():
                h_copy(u, way, 0, z).start()

    def h_pass(u, s):
        for way in range(2):
            @pl.when(has_source(way, s) & has_next(way))
            def _():
                h_copy(u, way, s - 1, source(way, s)).wait_recv()
                h_copy(u, way, s, source(way, s)).start()

    def h_keep(u, s):
        for way in range(2):
            @pl.when(has_source(way, s) & (z == (n_wide - 1 if way == 0 else 0)))
            def _():
                h_copy(u, way, s - 1, source(way, s)).wait_recv()

    def slot(g, c, h):
        return kbuf.at[pl.ds(pl.multiple_of((xor(chip, g, chips) * 2 + c) * kcols + h * hh, hh), hh)]

    def k_copy(g, h, held, to):
        ref = slot(held, core, h)
        return pltpu.make_async_remote_copy(
            src_ref=ref, dst_ref=ref, send_sem=k_send.at[g, h], recv_sem=k_recv.at[g, h],
            device_id=chip_at(to), device_id_type=MESH)

    def k_sent(g, h):
        return k_copy(g, h, 1 + h, 2 - h) if tree and g == 3 else k_copy(g, h, 0, g)

    def sib_copy(g, h, c):
        ref = slot(g, c, h)
        return pltpu.make_async_remote_copy(
            src_ref=ref, dst_ref=ref, send_sem=s_send.at[g, h], recv_sem=s_recv.at[g, h],
            device_id=at(z, chip * 2 + 1 - core), device_id_type=MESH)

    def k_arrive(g, h):
        k_copy(g, h, g, 1).wait_recv()
        if tree and g == 1 + h:
            k_sent(3, h).start()
        sib_copy(g, h, core).start()

    for u in range(n_wide - 1):
        h_own(u)
    tables[1].wait()
    load_k.wait()
    for b in range(tile_rows):
        k_in[tile_span(b), :] = k_in[tile_span(b), :] * mask_rows(ktiles, b, kcols)
    unit = lax.broadcasted_iota(jnp.int32, (kcols, kcols), 0) == lax.broadcasted_iota(jnp.int32, (kcols, kcols), 1)
    kbuf[pl.ds(pl.multiple_of(n * kcols, kcols), kcols), :] = turn(bf(unit), k_in[...])
    order = ((1, 0), (2, 1), (1, 1), (2, 0)) if tree else tuple((g, h) for g in direct for h in range(2))
    for g, h in order:
        k_sent(g, h).start()
    for h in range(2):
        sib_copy(0, h, core).start()
    out = turn(choose, h_in[...])
    for g in range(groups):
        full[g, :, pl.ds(pl.multiple_of(z * hrows, hrows), hrows)] = out[2 * g * tile:2 * (g + 1) * tile]

    kernel_steps = [order[:2], order[2:]] + ([((3, 0), (3, 1))] if tree else [])
    for s in range(1, n_wide - 1):
        for u in range(n_wide - 1):
            h_pass(u, s)
            if kernel_steps and (u, s) in ((0, 1), (1, 1), (0, 2)):
                for g, h in kernel_steps.pop(0):
                    k_arrive(g, h)
    for steps in kernel_steps:
        for g, h in steps:
            k_arrive(g, h)

    first_near = z // (n_wide - 1)
    far = (n_wide - 1) * (1 - first_near)

    upper = z // (n_wide // 2)
    lane = lax.broadcasted_iota(jnp.int32, (1, lanes), 1)
    low = lane < tile

    def group(i):
        return upper * i + (1 - upper) * (groups - 1 - i)

    def product(g, w, count):
        span = pl.ds(pl.multiple_of(w * hrows, hrows), count * hrows)
        return jnp.dot(full[g, :, span], kbuf[span, :], preferred_element_type=jnp.float32)

    def keeps(i):
        return (0,) if i == 0 else (2 * i - 1, 2 * i)

    def ready(i):
        for u in keeps(i):
            for s in range(1, n_wide - 1):
                h_keep(u, s)

        def step(w, carry):
            @pl.when(w != z)
            def _():
                unfold(group(i), w)

            return carry

        lax.fori_loop(first_near, first_near + n_wide - 1, step, 0)

    def slot_of(src, dst):
        return (src - dst + n_wide) % n_wide - 1

    own_copy = pltpu.make_async_copy(own, own_out, own_sem)

    def r_copy(i, k):
        there = slot_of(z, 2 * group(i) + k)
        return pltpu.make_async_remote_copy(
            src_ref=stage.at[2 * i + k], dst_ref=landed.at[there], send_sem=r_send.at[2 * i + k], recv_sem=r_recv.at[there],
            device_id=at(2 * group(i) + k, n), device_id_type=MESH)

    def r_wait(s):
        pltpu.make_async_remote_copy(
            src_ref=stage.at[0], dst_ref=landed.at[s - 1], send_sem=r_send.at[0], recv_sem=r_recv.at[s - 1],
            device_id=at((z + s) % n_wide, n), device_id_type=MESH).wait_recv()

    def finish(i):
        g = group(i)
        for b2 in range(tile_rows // 2):
            x = acc[:, lanes * b2:lanes * (b2 + 1)]
            y = pltpu.roll(x, tile, 1)
            table[2 * b2] = jnp.where(low, x, y).astype(jnp.bfloat16)
            table[2 * b2 + 1] = jnp.where(low, y, x).astype(jnp.bfloat16)

        def place(t):
            to = [owner[0, cols[2 * t + side]] for side in range(2)]
            at_lane = pl.ds(t * lanes, lanes)
            for k in range(2):
                kept = [(one == 2 * g + k).astype(jnp.int32) for one in to]
                left = jnp.where(low, kept[0], 0).astype(jnp.float32).astype(jnp.bfloat16)
                right = jnp.where(low, 0, kept[1]).astype(jnp.float32).astype(jnp.bfloat16)
                span = pl.ds(k * tile, tile)
                lhs[span, at_lane] = table[rows[2 * t], span] * left + table[rows[2 * t + 1], span] * right

        for t in range(pairs // 2):
            place(t)
        return jnp.dot(lhs[...], phi[...], preferred_element_type=jnp.float32)

    def chunk(i):
        if i > 0:
            @pl.when((z == 0) | (z == n_wide - 1))
            def _():
                ready(i)

        g = group(i)
        acc[...] = product(g, first_near, n_wide - 1)
        for u in keeps(i):
            h_keep(u, n_wide - 1)
        unfold(g, far)
        acc[...] += product(g, far, 1)
        blocks = finish(i)
        for k in range(2):
            block = blocks[k * tile:(k + 1) * tile]

            @pl.when(2 * g + k == z)
            def _():
                own[...] = block
                own_copy.start()

            @pl.when(2 * g + k != z)
            def _():
                stage[2 * i + k] = block.astype(jnp.bfloat16)
                r_copy(i, k).start()

    ready(0)

    @pl.when((z > 0) & (z < n_wide - 1))
    def _():
        for i in range(1, groups):
            ready(i)

    for g in range(chips):
        for h in range(2):
            sib_copy(g, h, 1 - core).wait_recv()
    load_p.wait()
    for load in tables[2:4]:
        load.wait()
    for i in range(groups):
        chunk(i)

    own_copy.wait()
    for s in range(1, n_wide):
        r_wait(s)

    for i in range(groups):
        for k in range(2):
            @pl.when(2 * group(i) + k != z)
            def _():
                r_copy(i, k).wait_send()
    for g in range(1, chips):
        for h in range(2):
            k_sent(g, h).wait_send()
    for g in range(chips):
        for h in range(2):
            sib_copy(g, h, core).wait_send()
    for u in range(n_wide - 1):
        for way in range(2):
            for s in range(n_wide - 1):
                @pl.when(has_next(way) & has_source(way, s))
                def _():
                    h_copy(u, way, s, source(way, s)).wait_send()


def body(n_wide, n_narrow, kernel, hamiltonian, kernel_tiles, ham_tiles, pair_row, pair_col, sphere_phi, owner):
    pairs, tile, pts = sphere_phi.shape
    height, kcols = kernel.shape
    hrows, breadth = hamiltonian.shape
    tile_rows, tile_cols = ham_tiles.shape
    chips = n_narrow // 2
    hbm = pl.BlockSpec(memory_space=pltpu.HBM)
    dma = pltpu.SemaphoreType.DMA
    unit_rows = (tile_rows // 2 - 1) * tile + tile // 2
    bf16 = jnp.bfloat16

    own, landed = pl.pallas_call(
        functools.partial(kernel_body, n_wide, n_narrow, tile),
        out_shape=(
            jax.ShapeDtypeStruct((tile, pts), jnp.float32),
            jax.ShapeDtypeStruct((n_wide - 1, tile, pts), bf16)),
        in_specs=[hbm] * 8,
        out_specs=(hbm, hbm),
        scratch_shapes=[
            pltpu.SMEM((tile_cols, tile_rows), jnp.int32),
            pltpu.SMEM((tile_cols, tile_rows), jnp.int32),
            pltpu.SMEM((pairs,), jnp.int32),
            pltpu.SMEM((pairs,), jnp.int32),
            pltpu.SMEM((1, tile_cols), jnp.int32),
            pltpu.VMEM((height, kcols), bf16),
            pltpu.VMEM((hrows, breadth), bf16),
            pltpu.VMEM((hrows, breadth), bf16),
            pltpu.VMEM((pairs * tile, pts), bf16),
            pltpu.VMEM((n_narrow * kcols, height), bf16),
            pltpu.VMEM((n_wide // 2, 2 * tile, n_wide * hrows), bf16),
            pltpu.VMEM((n_wide, n_wide * unit_rows + 2 * NOTE, 2 * tile), bf16),
            pltpu.VMEM((2 * tile, height), jnp.float32),
            pltpu.VMEM((tile_rows, 2 * tile, 2 * tile), bf16),
            pltpu.VMEM((2 * tile, pairs * tile), bf16),
            pltpu.VMEM((tile, pts), jnp.float32),
            pltpu.VMEM((n_wide, tile, pts), bf16),
            dma((8,)), dma(()),
            dma((chips, 2)), dma((chips, 2)),
            dma((chips, 2)), dma((chips, 2)),
            dma((n_wide, 2, n_wide)), dma((n_wide, 2, n_wide)),
            dma((n_wide,)), dma((n_wide,)),
        ],
        compiler_params=pltpu.CompilerParams(
            collective_id=0, has_side_effects=True, vmem_limit_bytes=60 * 2**20),
    )(kernel_tiles.T, ham_tiles.T, pair_row, pair_col, owner, kernel, hamiltonian,
      sphere_phi.reshape(pairs * tile, pts))
    for s in range(n_wide - 1):
        own = own + landed[s].astype(jnp.float32)
    return own[None]


def solution(mesh):
    return jax.shard_map(
        functools.partial(body, mesh.shape["wide"], mesh.shape["narrow"]),
        mesh=mesh,
        in_specs=(
            P("wide", "narrow"),
            P("wide", "narrow"),
            P("wide", "narrow"),
            P("wide", "narrow"),
            P(("wide", "narrow")),
            P(("wide", "narrow")),
            P(("wide", "narrow"), None, None),
            P("narrow", None),
        ),
        out_specs=P(("wide", "narrow"), None, None),
        check_vma=False,
    )
```
